512 devices in a mesh: ha: 16 (over x, y_lo), wa: 32 (over y_hi, z, core).
Axes of the slice: x: 4, y: 8 (y_hi: 2, y_lo: 4; y = y_hi * 4 + y_lo), z: 8, core: 2. Of those that a mesh axis runs over, the one named last changes fastest.
Arguments:
- velocity: float32 [2, 1024, 4096], P(None, 'wa', 'ha'), may hold values from -6 to 6
- cotangent: float32 [2, 1024, 4096], P(None, 'wa', 'ha'), may hold values from -6 to 6
- lift_weight: float32 [64, 2], replicated, may hold values from -4 to 4
- depth_kernels: float32 [1, 64, 9], replicated, may hold values from -2 to 2
- point_weights: bfloat16 [1, 64, 64], replicated, may hold values from -0.75 to 0.75
- out_weight: bfloat16 [2, 64], replicated, may hold values from -0.75 to 0.75
Outputs:
- grad_velocity: float32 [2, 1024, 4096], P(None, 'wa', 'ha')
- grad_lift: float32 [64, 2], replicated
- grad_kernels: float32 [1, 64, 9], replicated
- grad_point: float32 [1, 64, 64], replicated
- grad_out: float32 [2, 64], replicated
The draws below stay inside these ranges and needn't reach their ends.
All inputs are finite; a program needn't handle non-finite values.
Results may differ from the reference program's by a relative error of at most 0.012.
Values may be sent and summed in bfloat16 or wider, within the bound.
No kernel may reach another device: no remote copies, remote signals or barrier semaphores. Data moves between devices by JAX's collectives and lax.ppermute only.
A program may use at most 64 MiB of HBM per device.

```python
import math
import jax
import jax.numpy as jnp
from jax import lax

C = 64
LAYERS = 1
CW = 32
NX = 1024
NY = 4096


def steps_of(own_key, extent, split, smallest, high):
    def one(position, shards_of):
        draws = jax.random.uniform(jax.random.fold_in(jax.random.fold_in(own_key, 6), position), (shards_of,), jnp.float32, smallest / len(split), high / len(split))
        return jnp.repeat(jnp.exp(draws), extent[position] // shards_of).reshape((-1,) + (1,) * (len(extent) - position - 1))

    level = one(*split[0])
    for cut in split[1:]:
        level = level * one(*cut)
    return level


def gaussian(own_key, dims, scale, reach, split=(), kind=jnp.bfloat16):
    loudness = steps_of(own_key, dims, split, -0.22, 0.18) if split else 1.0
    values = jax.random.normal(own_key, dims, jnp.float32) * scale * loudness
    return jnp.minimum(jnp.maximum(values, -reach), reach).astype(kind)


def setup_inputs(seed: int = 0) -> dict:
    splits = jax.random.split(jax.random.key(seed), 7)
    velocity = gaussian(splits[0], (2, NX, NY), 1.0, 6.0, ((1, 32), (2, 16)), jnp.float32)
    cotangent = gaussian(splits[1], (2, NX, NY), 1.0, 6.0, ((1, 32), (2, 16)), jnp.float32)
    lift_weight = gaussian(splits[2], (C, 2), 2 ** -0.5, 4.0, (), jnp.float32)
    depth_kernels = gaussian(splits[3], (LAYERS, C, 9), 9 ** -0.5, 2.0, (), jnp.float32)
    point_weights = gaussian(splits[4], (LAYERS, C, C), C ** -0.5, 0.75)
    out_weight = gaussian(splits[5], (2, C), C ** -0.5, 0.75)
    return dict(velocity=velocity, cotangent=cotangent, lift_weight=lift_weight, depth_kernels=depth_kernels, point_weights=point_weights, out_weight=out_weight)


OFFSETS = ((-1, -1), (-1, 0), (-1, 1), (0, -1), (0, 0), (0, 1), (1, -1), (1, 0), (1, 1))

def signed_waves(count_n):
    ids = jnp.arange(count_n, dtype=jnp.int32)
    return jnp.where(2 * ids >= count_n, ids - count_n, ids).astype(jnp.float32)

def shifted(values, step_x, step_y):
    return jnp.roll(values, (-step_x, -step_y), axis=(1, 2))

def reference(velocity, cotangent, lift_weight, depth_kernels, point_weights, out_weight):
    highest = lax.Precision.HIGHEST
    spectrum = jnp.fft.fft2(cotangent, axes=(1, 2))
    wave_x = signed_waves(NX)[:, None]
    wave_y = signed_waves(NY)[None, :]
    along_k = wave_x * spectrum[0] + wave_y * spectrum[1]
    factor = along_k / jnp.maximum(wave_x * wave_x + wave_y * wave_y, 1.0)
    projected = jnp.stack([spectrum[0] - wave_x * factor, spectrum[1] - wave_y * factor])
    grad_proj = jnp.real(jnp.fft.ifft2(projected, axes=(1, 2))).astype(jnp.float32)
    margin = 2 * LAYERS
    extent_rows = CW + 2 * margin
    point_full = point_weights.astype(jnp.float32)
    out_full = out_weight.astype(jnp.float32)

    def band(totals, band_index):
        row_ids = (band_index * CW - margin + jnp.arange(extent_rows, dtype=jnp.int32)) % NX
        field_band = jnp.take(velocity, row_ids, axis=1)
        grad_band = jnp.take(grad_proj, row_ids, axis=1)
        hidden = jnp.einsum('cs,sxy->cxy', lift_weight, field_band, precision=highest).astype(jnp.bfloat16)
        saved_in, saved_depth, saved_tanh = ([], [], [])
        for layer_id in range(LAYERS):
            depth_acc = jnp.zeros(hidden.shape, jnp.float32)
            for offset_id in range(9):
                step_x, step_y = OFFSETS[offset_id]
                depth_acc = depth_acc + depth_kernels[layer_id, :, offset_id][:, None, None] * shifted(hidden, step_x, step_y).astype(jnp.float32)
            depth_out = depth_acc.astype(jnp.bfloat16)
            mixed_pre = jnp.einsum('oc,cxy->oxy', point_full[layer_id], depth_out.astype(jnp.float32), precision=highest)
            squash = jnp.tanh(mixed_pre).astype(jnp.bfloat16)
            saved_in.append(hidden)
            saved_depth.append(depth_out)
            saved_tanh.append(squash)
            hidden = (hidden.astype(jnp.float32) + squash.astype(jnp.float32)).astype(jnp.bfloat16)
        grad_b = grad_band.astype(jnp.bfloat16).astype(jnp.float32)
        lo_row = margin
        hi_row = margin + CW
        out_sum = jnp.einsum('sxy,cxy->sc', grad_b[:, lo_row:hi_row], hidden[:, lo_row:hi_row].astype(jnp.float32), precision=highest)
        grad_hidden = jnp.einsum('sc,sxy->cxy', out_full, grad_b, precision=highest)
        kernel_sums = [None] * LAYERS
        point_sums = [None] * LAYERS
        for layer_id in reversed(range(LAYERS)):
            squash_full = saved_tanh[layer_id].astype(jnp.float32)
            grad_mixed = (grad_hidden * (1.0 - squash_full * squash_full)).astype(jnp.bfloat16).astype(jnp.float32)
            point_sums[layer_id] = jnp.einsum('oxy,cxy->oc', grad_mixed[:, lo_row:hi_row], saved_depth[layer_id][:, lo_row:hi_row].astype(jnp.float32), precision=highest)
            grad_depth = jnp.einsum('oc,oxy->cxy', point_full[layer_id], grad_mixed, precision=highest).astype(jnp.bfloat16).astype(jnp.float32)
            entries = []
            for offset_id in range(9):
                step_x, step_y = OFFSETS[offset_id]
                moved_in = shifted(saved_in[layer_id], step_x, step_y).astype(jnp.float32)
                entries.append(lax.optimization_barrier(jnp.sum(grad_depth[:, lo_row:hi_row] * moved_in[:, lo_row:hi_row], axis=(1, 2))))
                grad_hidden = grad_hidden + depth_kernels[layer_id, :, offset_id][:, None, None] * jnp.roll(grad_depth, (step_x, step_y), axis=(1, 2))
            kernel_sums[layer_id] = jnp.stack(entries, axis=1)
        lift_sum = jnp.einsum('cxy,sxy->cs', grad_hidden[:, lo_row:hi_row], field_band[:, lo_row:hi_row], precision=highest)
        grad_rows = grad_band[:, lo_row:hi_row] + jnp.einsum('cs,cxy->sxy', lift_weight, grad_hidden[:, lo_row:hi_row], precision=highest)
        new_totals = (totals[0] + lift_sum, totals[1] + jnp.stack(kernel_sums), totals[2] + jnp.stack(point_sums), totals[3] + out_sum)
        return (new_totals, grad_rows)
    start = (jnp.zeros((C, 2), jnp.float32), jnp.zeros((LAYERS, C, 9), jnp.float32), jnp.zeros((LAYERS, C, C), jnp.float32), jnp.zeros((2, C), jnp.float32))
    totals, bands = lax.scan(band, start, jnp.arange(NX // CW, dtype=jnp.int32))
    grad_velocity = jnp.transpose(bands, (1, 0, 2, 3)).reshape(2, NX, NY)
    scale = 1.0 / math.sqrt(NX * NY)
    return (grad_velocity, totals[0] * scale, totals[1] * scale, totals[2] * scale, totals[3] * scale)
```

```python
import math

import jax
import jax.numpy as jnp
import ml_dtypes
import numpy as np
from jax import lax
from jax.experimental import pallas as pl
from jax.experimental.pallas import tpu as pltpu
from jax.sharding import PartitionSpec as P

BF = jnp.bfloat16
F32 = jnp.float32
HA, WA = 16, 32
ROWS, COLS = 32, 256
NX, NY = WA * ROWS, HA * COLS
TWO_PI = 2.0 * math.pi
COL_ID = np.concatenate([np.arange(256), [-1, 256]])


def bf(table):
    return np.asarray(table).astype(ml_dtypes.bfloat16)


def pair(table):
    high = bf(table)
    return np.stack([high, bf(table - high.astype(np.float64))])


def make_tables():
    r = np.arange(256)
    k2 = np.arange(128)
    ang = TWO_PI * (np.outer(k2, r) % 256) / 256
    c, s = np.cos(ang), np.sin(ang)
    t1 = np.stack([np.concatenate([c, s], 1), np.concatenate([-s, c], 1)], 1)
    t1 = t1.reshape(32, 4, 2, 512).transpose(1, 0, 2, 3).reshape(256, 512)

    n32 = np.arange(32)
    a32 = TWO_PI * (np.outer(n32, n32) % 32) / 32
    c32, s32 = np.cos(a32), np.sin(a32)
    d1 = np.zeros((4, 32, 32, 2))
    d1[0, :, :, 0] = c32
    d1[1, :, :, 0] = -s32
    d1[2, :, :, 1] = c32
    d1[3, :, :, 1] = -s32
    d1 = d1.reshape(128, 64)
    tw = TWO_PI * np.outer(n32, np.tile(n32, 8)) / 1024
    tw1 = np.stack([np.cos(tw), np.sin(tw)]).astype(np.float32)

    kr = np.zeros((2, 4, 32, 2, 4, 32))
    ik = np.zeros((2, 4, 32, 2, 256))
    rows = np.concatenate([n32, [-1, 32]])
    a = TWO_PI * np.outer(n32, rows) / 32
    row_of = np.zeros(256)
    for j in range(4):
        kr[0, j, :, 0, j, :] = c32
        kr[1, j, :, 0, j, :] = s32
        kr[1, j, :, 1, j, :] = c32
        kr[0, j, :, 1, j, :] = -s32
        lanes = list(range(j * 32, j * 32 + 32)) + [128 + j * 2, 129 + j * 2]
        row_of[lanes] = rows
        ik[0, j, :, 0, lanes] = np.cos(a).T
        ik[1, j, :, 0, lanes] = -np.sin(a).T
        ik[0, j, :, 1, lanes] = np.sin(a).T
        ik[1, j, :, 1, lanes] = np.cos(a).T
    kr = kr.reshape(256, 256)
    ik = ik.reshape(256, 512)
    tw = TWO_PI * np.outer(n32, row_of) / 1024
    tw2 = np.stack([np.cos(tw), np.sin(tw)]).astype(np.float32)
    d2 = np.zeros((32, 2, 2, 32))
    d2[:, 0, 0] = c32
    d2[:, 0, 1] = -s32
    d2[:, 1, 0] = s32
    d2[:, 1, 1] = c32
    d2 = d2.reshape(64, 64)

    ang = TWO_PI * (np.outer(k2, COL_ID) % 256) / 256
    tk = np.zeros((128, 2, 2, 384))
    tk[:, 0, 0, :258] = 2 * np.cos(ang)
    tk[:, 1, 0, :258] = -2 * np.sin(ang)
    tk[:, 0, 1, :258] = 2 * np.sin(ang)
    tk[:, 1, 1, :258] = 2 * np.cos(ang)
    tk = tk.reshape(32, 4, 2, 768).transpose(1, 0, 2, 3).reshape(256, 768)
    return dict(t1=pair(t1), d1=pair(d1), tw1=tw1, kr=pair(kr), ik=pair(ik), tw2=tw2, d2=pair(d2), tk=pair(tk))


def mm(a, b, ca=1, cb=0):
    return lax.dot_general(a, b, (((ca,), (cb,)), ((), ())), preferred_element_type=F32)


def halves(value):
    high = value.astype(BF)
    return high, (value - high.astype(F32)).astype(BF)


def mm3(a, b, ca=1, cb=0):
    return mm(a[0], b[0], ca, cb) + (mm(a[1], b[0], ca, cb) + mm(a[0], b[1], ca, cb))


def y_forward(got, turn, sign, t1):
    re = jnp.zeros((64, 256), F32)
    im = jnp.zeros((64, 256), F32)
    for q in range(HA):
        part = got[q, :64].astype(F32)
        re = re + part * turn[0, q : q + 1]
        im = im - part * turn[1, q : q + 1]
    both = halves(jnp.concatenate([re, im], axis=1))
    row = lax.broadcasted_iota(jnp.int32, (64, 256), 0)
    pick = jnp.where(row == 1, sign, 0.0).astype(BF)
    out = []
    for j in range(4):
        block = mm3((t1[0, j * 64 : (j + 1) * 64], t1[1, j * 64 : (j + 1) * 64]), both, 1, 1)
        if j == 0:
            block = block + mm(pick, both[0][:, :256], 1, 1) + mm(pick, both[1][:, :256], 1, 1)
        out.append(block)
    pieces = [out[j][:, 32 * c : 32 * c + 32] for c in range(2) for j in range(4)]
    return jnp.concatenate(pieces, axis=1).astype(BF)


def x_project(lines, ky_lane, d1, tw1, kr, ik, tw2, d2):
    first = mm(d1[0], lines) + mm(d1[1], lines)
    cs, sn = tw1[0], tw1[1]
    turned = []
    for c in range(2):
        for p in range(2):
            re = first[64 * p : 64 * p + 32]
            im = first[64 * p + 32 : 64 * p + 64]
            span = slice(128 * c, 128 * c + 128)
            turned.append(
                jnp.concatenate([(re * cs + im * sn)[:, span], (im * cs - re * sn)[:, span]], axis=1)
            )
    spec = mm3(halves(jnp.concatenate(turned, axis=0)), kr)
    lane = lax.broadcasted_iota(jnp.int32, (32, 128), 1)
    kx = lax.broadcasted_iota(jnp.int32, (32, 128), 0) + 32 * (lane % 32)
    kx = jnp.where(2 * kx >= NX, kx - NX, kx).astype(F32)
    ky = jnp.broadcast_to(ky_lane, (32, 128))
    edge_x = kx == -float(NX // 2)

    def factors(wave_y, edge_y):
        inv = 1.0 / jnp.maximum(kx * kx + wave_y * wave_y, 1.0)
        scale = 1.0 / float(NX * NY)
        cross = jnp.where(edge_x != edge_y, 0.0, -kx * wave_y * inv)
        return (1.0 - kx * kx * inv) * scale, cross * scale, (1.0 - wave_y * wave_y * inv) * scale

    ar, br, dr = factors(ky, jnp.zeros((32, 128), jnp.bool_))
    packed = ky == 0.0
    ai, bi, di = factors(jnp.where(packed, -float(NY // 2), ky), packed)
    (r0, r0i), (i0, i0i), (r1, r1i), (i1, i1i) = (
        (spec[32 * i : 32 * i + 32, :128], spec[32 * i : 32 * i + 32, 128:]) for i in range(4)
    )
    first = jnp.concatenate(
        [ar * r0 + br * r1 - (ai * i0i + bi * i1i), ar * r0i + br * r1i + ai * i0 + bi * i1], axis=1
    )
    second = jnp.concatenate(
        [br * r0 + dr * r1 - (bi * i0i + di * i1i), br * r0i + dr * r1i + bi * i0 + di * i1], axis=1
    )
    back = mm3(halves(jnp.concatenate([first, second], axis=0)), ik)
    cs, sn = tw2[0], tw2[1]
    main, rim = [], []
    for c in range(2):
        re = back[32 * c : 32 * c + 32, :256]
        im = back[32 * c : 32 * c + 32, 256:]
        value = jnp.concatenate([re * cs - im * sn, re * sn + im * cs], axis=0)
        main.append(value[:, :128])
        rim.append(value[:, 128:136])
    stack = jnp.concatenate(main + rim + [jnp.zeros((64, 112), F32)], axis=1)
    return mm3(d2, halves(stack)).astype(BF)


def regroup(lines):
    a = lax.broadcasted_iota(jnp.int32, (64, 64), 0)
    b = lax.broadcasted_iota(jnp.int32, (64, 64), 1)
    eye = jnp.where(a == b, 1.0, 0.0).astype(BF)
    turned = mm(lines, eye, 0, 0)
    main = jnp.concatenate(
        [
            jnp.concatenate([turned[32 * j : 32 * j + 32] for j in range(4)], axis=1),
            jnp.concatenate([turned[128 + 32 * j : 160 + 32 * j] for j in range(4)], axis=1),
        ],
        axis=0,
    )
    rim = jnp.concatenate(
        [jnp.concatenate([turned[256 + 8 * c + 2 * j : 258 + 8 * c + 2 * j] for j in range(4)], axis=1) for c in range(2)],
        axis=0,
    )
    return jnp.concatenate([main, rim, jnp.zeros((12, 256), F32)], axis=0).astype(BF)


def y_inverse(got, turn, tk):
    lane = lax.broadcasted_iota(jnp.int32, (1, 384), 1)
    odd = jnp.where(lane < 256, lane % 2, (lane == 256).astype(jnp.int32)).astype(F32)
    own = got[0].astype(F32)
    acc = own[:, 1:2] * (1.0 - 2.0 * odd) - own[:, 0:1]
    acc = acc + mm(got[0], tk[0, :, :384]) + mm(got[0], tk[1, :, :384])
    for q in range(1, HA):
        part = mm(got[q], tk[0]) + mm(got[q], tk[1])
        acc = acc + part[:, :384] * turn[0, q : q + 1] - part[:, 384:] * turn[1, q : q + 1]
    return acc


def network(proj, planes, center, point, lift18, out_cols):
    mix = lax.dot_general(point, lift18, (((1,), (0,)), ((), ())), precision=lax.Precision.HIGHEST, preferred_element_type=F32)
    mix_b = mix.astype(BF)
    proj_b = proj.astype(BF).astype(F32)
    taps = [None] * 34
    sums = jnp.zeros((32, 128), F32)
    for i in range(-1, 33):
        view = planes[(i + 1) * 8 : (i + 4) * 8].astype(BF)
        t_b = jnp.tanh(mm(mix_b, view)).astype(BF)
        t = t_b.astype(F32)
        ids = (64, 66) if i < 0 else (65, 67) if i >= 32 else (i, 32 + i)
        g0 = proj_b[ids[0] : ids[0] + 1]
        g1 = proj_b[ids[1] : ids[1] + 1]
        grad = out_cols[:, 0:1] * g0 + out_cols[:, 1:2] * g1
        gz = (grad * (1.0 - t * t)).astype(BF)
        tap = mm(mix_b, gz, 0, 0)
        for a in range(3):
            k = i + a - 1
            if 0 <= k < 32:
                piece = tap[a * 8 : a * 8 + 8]
                taps[k] = piece if taps[k] is None else taps[k] + piece
        if 0 <= i < 32:
            g8 = jnp.concatenate([g0[:, :256], g1[:, :256], jnp.zeros((6, 256), F32)], axis=0).astype(BF)
            left = jnp.concatenate([view[:, :256], g8], axis=0)
            right = jnp.concatenate([gz[:, :256], t_b[:, :256]], axis=0)
            sums = sums + mm(left, right, 1, 1)
    tail = sums[24:32, 64:]
    row = lax.broadcasted_iota(jnp.int32, (8, 64), 0)
    lane = lax.broadcasted_iota(jnp.int32, (8, 64), 1)
    for s in range(2):
        for v in range(2):
            prod = proj_b[32 * s : 32 * s + 32, :256] * center[32 * v : 32 * v + 32]
            total = jnp.sum(jnp.sum(prod, axis=0, keepdims=True), axis=1, keepdims=True)
            tail = jnp.where((row == 2) & (lane == 2 * s + v), total, tail)
    packed = jnp.concatenate(
        [
            jnp.concatenate([sums[0:8, :64], sums[8:16, :64]], axis=1),
            jnp.concatenate([sums[16:24, :64], tail], axis=1),
        ],
        axis=0,
    )
    return jnp.concatenate(taps[:32], axis=0), packed


def call(body, out_shapes, *args):
    single = not isinstance(out_shapes, (tuple, list))

    def kernel(*refs):
        ins = [ref[...] for ref in refs[: len(args)]]
        outs = body(*ins)
        for ref, value in zip(refs[len(args) :], [outs] if single else outs):
            ref[...] = value

    return pl.pallas_call(
        kernel,
        out_shape=out_shapes,
        compiler_params=pltpu.CompilerParams(vmem_limit_bytes=40 * 1024 * 1024),
    )(*args)


def sds(shape, dtype):
    return jax.ShapeDtypeStruct(shape, dtype)


def everyone(value, axis, count):
    spread = jnp.broadcast_to(value[None], (count,) + value.shape)
    return lax.all_to_all(spread, axis, split_axis=0, concat_axis=0)


def prepare(velocity, cotangent):
    vel = velocity.astype(BF)
    edges = jnp.concatenate([vel[:, :, 0:2], vel[:, :, 254:256]], axis=2).reshape(1, 256)
    return jnp.concatenate(
        [cotangent.astype(BF).reshape(64, 256), edges, jnp.zeros((15, 256), BF)], axis=0
    )


def turns(own, cols):
    ang = TWO_PI / NY * (own * cols % NY).astype(F32)
    return jnp.stack([jnp.cos(ang), jnp.sin(ang)])


def wide(got, velocity, h):
    left = lax.dynamic_index_in_dim(got, (h + 15) % 16, 0, False)[64].reshape(2, 32, 4)
    right = lax.dynamic_index_in_dim(got, (h + 1) % 16, 0, False)[64].reshape(2, 32, 4)
    return jnp.concatenate([left[:, :, 2:4], velocity.astype(BF), right[:, :, 0:2]], axis=2)


def second_send(spec, vel_y, w):
    first, last = vel_y[:, :2], vel_y[:, 30:]

    def rows(v):
        v = v.reshape(4, 260)
        corner = jnp.concatenate([v[:, :2], v[:, 258:]], axis=1).reshape(1, 16)
        return jnp.concatenate(
            [v[:, 2:258], jnp.pad(corner, ((0, 0), (0, 240))), jnp.zeros((1, 256), BF)], axis=0
        )

    dest = jnp.arange(WA)[:, None, None]
    rims = jnp.where(dest == (w + 1) % WA, rows(last)[None], rows(first)[None])
    return jnp.concatenate([spec.reshape(32, 2, 256), rims], axis=1)


def velocity_planes(got2, vel_y, w):
    def rows(src):
        v = lax.dynamic_index_in_dim(got2, src, 0, False)[2:7]
        corner = v[4, :16].reshape(4, 4)
        v = jnp.concatenate([corner[:, :2], v[:4], corner[:, 2:]], axis=1)
        return v.reshape(2, 2, 260)

    full = jnp.concatenate([rows((w + 31) % WA), vel_y, rows((w + 1) % WA)], axis=1)
    moved = []
    for s in range(2):
        for b in (-1, 0, 1):
            v = full[s]
            moved.append(
                jnp.concatenate(
                    [v[:, 2 + b : 258 + b], v[:, 1 + b : 2 + b], v[:, 258 + b : 259 + b], jnp.zeros((36, 126), BF)],
                    axis=1,
                )
            )
    moved += [jnp.zeros((36, 384), BF)] * 2
    return jnp.stack(moved, axis=1).reshape(288, 384).astype(F32)


def lift_matrix(lift, kernels):
    parts = []
    for a in range(3):
        for s in range(2):
            for b in range(3):
                parts.append(kernels[:, 3 * a + b] * lift[:, s])
        parts += [jnp.zeros_like(parts[0])] * 2
    return jnp.stack(parts, axis=1)


def finish_velocity(proj, taps, lift, out_w):
    hi = lax.Precision.HIGHEST
    main = proj[:64, :256].reshape(2, 32, 256)
    main_b = main.astype(BF).astype(F32)
    m2 = jnp.dot(lift.T, out_w.astype(F32).T, precision=hi)
    taps = taps.reshape(32, 8, 384)
    out = []
    for s in range(2):
        left, mid, right = taps[:, 3 * s], taps[:, 3 * s + 1], taps[:, 3 * s + 2]
        value = main[s] + m2[s, 0] * main_b[0] + m2[s, 1] * main_b[1] + mid[:, :256]
        value = value + jnp.concatenate([right[:, 256:257], right[:, :255]], axis=1)
        value = value + jnp.concatenate([left[:, 1:256], left[:, 257:258]], axis=1)
        out.append(value)
    return jnp.stack(out)


def finish_weights(total, lift, kernels, point, out_w, lift18):
    hi = lax.Precision.HIGHEST
    scale = 1.0 / math.sqrt(NX * NY)
    total = total * scale
    q = jnp.concatenate([total[:8, :64], total[:8, 64:], total[8:, :64]], axis=0)
    gpt = total[8:10, 64:]
    gpv = total[10, 64:68].reshape(2, 2)
    grad_out = gpt + jnp.dot(gpv, lift.T, precision=hi)
    grad_point = jnp.einsum("ko,ck->oc", q, lift18, precision=hi)
    gv = jnp.einsum("ko,oc->ck", q, point.astype(F32), precision=hi)
    gv = gv.reshape(64, 3, 8)[:, :, :6].reshape(64, 3, 2, 3)
    grad_kernels = jnp.sum(gv * lift[:, None, :, None], axis=2).reshape(64, 9)
    grad_lift = jnp.sum(gv * kernels.reshape(64, 3, 1, 3), axis=(1, 3))
    grad_lift = grad_lift + jnp.dot(out_w.astype(F32).T, gpv, precision=hi)
    return grad_lift, grad_kernels[None], grad_point[None], grad_out


def local(velocity, cotangent, lift_weight, depth_kernels, point_weights, out_weight):
    tab = make_tables()
    h = lax.axis_index("ha")
    w = lax.axis_index("wa")
    kernels = depth_kernels[0]
    point = point_weights[0]
    col = jnp.arange(256)[None, :]
    peer = jnp.arange(HA)[:, None]
    turn1 = turns(h, col + 256 * peer)
    sign = jnp.where(h == 0, (1 - 2 * (col % 2)).astype(F32), 0.0)
    ky_lane = (h + 16 * (4 * w + jnp.arange(128) // 32)).astype(F32)[None, :]
    cols4 = jnp.asarray(np.concatenate([COL_ID, np.zeros(126, np.int64)]).astype(np.int32))[None, :]
    turn4 = turns(peer, cols4 + 256 * h + NY)
    lift18 = lift_matrix(lift_weight, kernels)

    got1 = everyone(prepare(velocity, cotangent), "ha", HA)
    spec = call(y_forward, sds((64, 256), BF), got1, turn1, sign, tab["t1"])
    vel_y = wide(got1, velocity, h)
    got2 = lax.all_to_all(second_send(spec, vel_y, w), "wa", split_axis=0, concat_axis=0)
    lines = got2[:, :2].reshape(64, 256)
    sent3 = call(
        x_project, sds((64, 384), BF), lines, ky_lane, tab["d1"], tab["tw1"], tab["kr"], tab["ik"], tab["tw2"], tab["d2"]
    )
    got3 = lax.all_to_all(sent3.reshape(32, 2, 384), "wa", split_axis=0, concat_axis=0)
    planes = velocity_planes(got2, vel_y, w)
    sent4 = call(regroup, sds((80, 256), BF), got3.reshape(64, 384))
    got4 = everyone(sent4, "ha", HA)

    def last(got, turn, tk, planes, center, point, lift18, out_cols):
        proj = y_inverse(got, turn, tk)
        taps, packed = network(proj, planes, center, point, lift18, out_cols)
        return proj, taps, packed

    proj, taps, packed = call(
        last,
        (sds((80, 384), F32), sds((256, 384), F32), sds((16, 128), F32)),
        got4, turn4, tab["tk"], planes, velocity.reshape(64, 256), point.astype(F32), lift18, out_weight.astype(F32).T,
    )
    part = jnp.sum(everyone(packed, "ha", HA), axis=0)
    total = jnp.sum(everyone(part, "wa", WA), axis=0)
    grad_velocity = finish_velocity(proj, taps, lift_weight, out_weight)
    return (grad_velocity,) + finish_weights(total, lift_weight, kernels, point, out_weight, lift18)


def solution(mesh):
    return jax.shard_map(
        local,
        mesh=mesh,
        in_specs=(P(None, "wa", "ha"), P(None, "wa", "ha"), P(), P(), P(), P()),
        out_specs=(P(None, "wa", "ha"), P(), P(), P(), P()),
        check_vma=False,
    )
```

```python
import math

import jax
import jax.numpy as jnp
import ml_dtypes
import numpy as np
from jax import lax
from jax.experimental import pallas as pl
from jax.experimental.pallas import tpu as pltpu
from jax.sharding import PartitionSpec as P

BF = jnp.bfloat16
F32 = jnp.float32
HA, WA = 16, 32
AXES = ("x", "yl", "yh", "z", "c")
SIZES = (4, 4, 2, 8, 2)
IN_H = ("x", "yl")
IN_W = ("yh", "z", "c")
ROWS, COLS = 32, 256
NX, NY = WA * ROWS, HA * COLS
TWO_PI = 2.0 * math.pi
COL_ID = np.concatenate([np.arange(256), [-1, 256]])


def bf(table):
    return np.asarray(table).astype(ml_dtypes.bfloat16)


def pair(table):
    high = bf(table)
    return np.stack([high, bf(table - high.astype(np.float64))])


def make_tables():
    r = np.arange(256)
    k2 = np.arange(128)
    ang = TWO_PI * (np.outer(k2, r) % 256) / 256
    c, s = np.cos(ang), np.sin(ang)
    t1 = np.stack([np.concatenate([c, s], 1), np.concatenate([-s, c], 1)], 1)
    t1 = t1.reshape(32, 4, 2, 512).transpose(1, 0, 2, 3).reshape(256, 512)

    n32 = np.arange(32)
    a32 = TWO_PI * (np.outer(n32, n32) % 32) / 32
    c32, s32 = np.cos(a32), np.sin(a32)
    d1 = np.zeros((4, 32, 32, 2))
    d1[0, :, :, 0] = c32
    d1[1, :, :, 0] = -s32
    d1[2, :, :, 1] = c32
    d1[3, :, :, 1] = -s32
    d1 = d1.reshape(128, 64)
    tw = TWO_PI * np.outer(n32, np.tile(n32, 8)) / 1024
    tw1 = np.stack([np.cos(tw), np.sin(tw)]).astype(np.float32)

    kr = np.zeros((2, 4, 32, 2, 4, 32))
    ik = np.zeros((2, 4, 32, 2, 256))
    rows = np.concatenate([n32, [-1, 32]])
    a = TWO_PI * np.outer(n32, rows) / 32
    row_of = np.zeros(256)
    for j in range(4):
        kr[0, j, :, 0, j, :] = c32
        kr[1, j, :, 0, j, :] = s32
        kr[1, j, :, 1, j, :] = c32
        kr[0, j, :, 1, j, :] = -s32
        lanes = list(range(j * 32, j * 32 + 32)) + [128 + j * 2, 129 + j * 2]
        row_of[lanes] = rows
        ik[0, j, :, 0, lanes] = np.cos(a).T
        ik[1, j, :, 0, lanes] = -np.sin(a).T
        ik[0, j, :, 1, lanes] = np.sin(a).T
        ik[1, j, :, 1, lanes] = np.cos(a).T
    kr = kr.reshape(256, 256)
    ik = ik.reshape(256, 512)
    tw = TWO_PI * np.outer(n32, row_of) / 1024
    tw2 = np.stack([np.cos(tw), np.sin(tw)]).astype(np.float32)
    d2 = np.zeros((32, 2, 2, 32))
    d2[:, 0, 0] = c32
    d2[:, 0, 1] = -s32
    d2[:, 1, 0] = s32
    d2[:, 1, 1] = c32
    d2 = d2.reshape(64, 64)

    ang = TWO_PI * (np.outer(k2, COL_ID) % 256) / 256
    tk = np.zeros((128, 2, 2, 384))
    tk[:, 0, 0, :258] = 2 * np.cos(ang)
    tk[:, 1, 0, :258] = -2 * np.sin(ang)
    tk[:, 0, 1, :258] = 2 * np.sin(ang)
    tk[:, 1, 1, :258] = 2 * np.cos(ang)
    tk = tk.reshape(32, 4, 2, 768).transpose(1, 0, 2, 3).reshape(256, 768)
    return dict(t1=pair(t1), d1=pair(d1), tw1=tw1, kr=pair(kr), ik=pair(ik), tw2=tw2, d2=pair(d2), tk=bf(tk))


def mm(a, b, ca=1, cb=0):
    return lax.dot_general(a, b, (((ca,), (cb,)), ((), ())), preferred_element_type=F32)


def halves(value):
    high = value.astype(BF)
    return high, (value - high.astype(F32)).astype(BF)


def mm3(a, b, ca=1, cb=0):
    return mm(a[0], b[0], ca, cb) + (mm(a[1], b[0], ca, cb) + mm(a[0], b[1], ca, cb))


def y_forward(got, turn, sign, t1):
    parts = [got[q, :64].astype(F32) for q in range(4)]
    row = lax.broadcasted_iota(jnp.int32, (64, 256), 0)
    pick = jnp.where(row == 1, sign, 0.0).astype(BF)
    result = []
    for e in range(4):
        re = sum(parts[q] * turn[0, 4 * e + q : 4 * e + q + 1] for q in range(4))
        im = -sum(parts[q] * turn[1, 4 * e + q : 4 * e + q + 1] for q in range(4))
        both = halves(jnp.concatenate([re, im], axis=1))
        out = []
        for j in range(4):
            block = mm3((t1[0, j * 64 : (j + 1) * 64], t1[1, j * 64 : (j + 1) * 64]), both, 1, 1)
            if e == 0 and j == 0:
                block = block + mm(pick, both[0][:, :256], 1, 1) + mm(pick, both[1][:, :256], 1, 1)
            out.append(block)
        pieces = [out[j][:, 32 * c : 32 * c + 32] for c in range(2) for j in range(4)]
        result.append(jnp.concatenate(pieces, axis=1).astype(BF))
    return jnp.concatenate(result, axis=0)


def x_project(lines, ky_lane, d1, tw1, kr, ik, tw2, d2):
    lines = lines.astype(F32)
    first = mm3(d1, halves((lines[0] + lines[1]) + (lines[2] + lines[3])))
    cs, sn = tw1[0], tw1[1]
    turned = []
    for c in range(2):
        for p in range(2):
            re = first[64 * p : 64 * p + 32]
            im = first[64 * p + 32 : 64 * p + 64]
            span = slice(128 * c, 128 * c + 128)
            turned.append(
                jnp.concatenate([(re * cs + im * sn)[:, span], (im * cs - re * sn)[:, span]], axis=1)
            )
    spec = mm3(halves(jnp.concatenate(turned, axis=0)), kr)
    lane = lax.broadcasted_iota(jnp.int32, (32, 128), 1)
    kx = lax.broadcasted_iota(jnp.int32, (32, 128), 0) + 32 * (lane % 32)
    kx = jnp.where(2 * kx >= NX, kx - NX, kx).astype(F32)
    ky = jnp.broadcast_to(ky_lane, (32, 128))
    edge_x = kx == -float(NX // 2)

    def factors(wave_y, edge_y):
        inv = 1.0 / jnp.maximum(kx * kx + wave_y * wave_y, 1.0)
        scale = 1.0 / float(NX * NY)
        cross = jnp.where(edge_x != edge_y, 0.0, -kx * wave_y * inv)
        return (1.0 - kx * kx * inv) * scale, cross * scale, (1.0 - wave_y * wave_y * inv) * scale

    ar, br, dr = factors(ky, jnp.zeros((32, 128), jnp.bool_))
    packed = ky == 0.0
    ai, bi, di = factors(jnp.where(packed, -float(NY // 2), ky), packed)
    (r0, r0i), (i0, i0i), (r1, r1i), (i1, i1i) = (
        (spec[32 * i : 32 * i + 32, :128], spec[32 * i : 32 * i + 32, 128:]) for i in range(4)
    )
    first = jnp.concatenate(
        [ar * r0 + br * r1 - (ai * i0i + bi * i1i), ar * r0i + br * r1i + ai * i0 + bi * i1], axis=1
    )
    second = jnp.concatenate(
        [br * r0 + dr * r1 - (bi * i0i + di * i1i), br * r0i + dr * r1i + bi * i0 + di * i1], axis=1
    )
    back = mm3(halves(jnp.concatenate([first, second], axis=0)), ik)
    cs, sn = tw2[0], tw2[1]
    main, rim = [], []
    for c in range(2):
        re = back[32 * c : 32 * c + 32, :256]
        im = back[32 * c : 32 * c + 32, 256:]
        value = jnp.concatenate([re * cs - im * sn, re * sn + im * cs], axis=0)
        main.append(value[:, :128])
        rim.append(value[:, 128:136])
    stack = jnp.concatenate(main + rim + [jnp.zeros((64, 112), F32)], axis=1)
    return mm3(d2, halves(stack)).astype(BF)


def regroup(lines):
    a = lax.broadcasted_iota(jnp.int32, (64, 64), 0)
    b = lax.broadcasted_iota(jnp.int32, (64, 64), 1)
    eye = jnp.where(a == b, 1.0, 0.0).astype(BF)
    turned = mm(lines, eye, 0, 0)
    main = jnp.concatenate(
        [
            jnp.concatenate([turned[32 * j : 32 * j + 32] for j in range(4)], axis=1),
            jnp.concatenate([turned[128 + 32 * j : 160 + 32 * j] for j in range(4)], axis=1),
        ],
        axis=0,
    )
    rim = jnp.concatenate(
        [jnp.concatenate([turned[256 + 8 * c + 2 * j : 258 + 8 * c + 2 * j] for j in range(4)], axis=1) for c in range(2)],
        axis=0,
    )
    return jnp.concatenate([main, rim, jnp.zeros((4, 256), F32)], axis=0).astype(BF)


def y_inverse(got, turn, zero, tk):
    lane = lax.broadcasted_iota(jnp.int32, (1, 384), 1)
    odd = jnp.where(lane < 256, lane % 2, (lane == 256).astype(jnp.int32)).astype(F32)
    acc = [None] * 4
    for e in range(4):
        lines = regroup(got[e])
        part = mm(lines, tk)
        re, im = part[:, :384], part[:, 384:]
        if e == 0:
            own = lines.astype(F32)
            once = zero * (own[:, 1:2] * (1.0 - 2.0 * odd) - own[:, 0:1])
        for d in range(4):
            i = 4 * e + d
            piece = re * turn[0, i : i + 1] - im * turn[1, i : i + 1]
            acc[d] = piece + once if e == 0 else acc[d] + piece
    return jnp.concatenate(acc, axis=0).astype(BF)


def network(proj, planes, center, point, lift18, out_cols):
    mix = lax.dot_general(point, lift18, (((1,), (0,)), ((), ())), precision=lax.Precision.HIGHEST, preferred_element_type=F32)
    mix_hi, mix_lo = halves(mix)
    mix3 = jnp.concatenate([mix_hi, mix_lo, mix_hi], axis=1)
    mix2 = mix3[:, :48]
    proj_b = proj.astype(BF).astype(F32)
    taps = [None] * 34
    sums = jnp.zeros((56, 128), F32)
    for i in range(-1, 33):
        view, view_lo = halves(planes[(i + 1) * 8 : (i + 4) * 8])
        t_b = jnp.tanh(mm(mix3, jnp.concatenate([view, view, view_lo], axis=0))).astype(BF)
        t = t_b.astype(F32)
        ids = (64, 66) if i < 0 else (65, 67) if i >= 32 else (i, 32 + i)
        g0 = proj_b[ids[0] : ids[0] + 1]
        g1 = proj_b[ids[1] : ids[1] + 1]
        grad = out_cols[:, 0:1] * g0 + out_cols[:, 1:2] * g1
        gz = (grad * (1.0 - t * t)).astype(BF)
        tap = mm(mix2, gz, 0, 0)
        tap = tap[:24] + tap[24:]
        for a in range(3):
            k = i + a - 1
            if 0 <= k < 32:
                piece = tap[a * 8 : a * 8 + 8]
                taps[k] = piece if taps[k] is None else taps[k] + piece
        if 0 <= i < 32:
            g8 = jnp.concatenate([g0[:, :256], g1[:, :256], jnp.zeros((6, 256), F32)], axis=0).astype(BF)
            left = jnp.concatenate([view[:, :256], view_lo[:, :256], g8], axis=0)
            right = jnp.concatenate([gz[:, :256], t_b[:, :256]], axis=0)
            sums = sums + mm(left, right, 1, 1)
    tail = sums[48:56, 64:]
    sums = sums[:24] + sums[24:48]
    row = lax.broadcasted_iota(jnp.int32, (8, 64), 0)
    lane = lax.broadcasted_iota(jnp.int32, (8, 64), 1)
    for s in range(2):
        for v in range(2):
            prod = proj_b[32 * s : 32 * s + 32, :256] * center[32 * v : 32 * v + 32]
            total = jnp.sum(jnp.sum(prod, axis=0, keepdims=True), axis=1, keepdims=True)
            tail = jnp.where((row == 2) & (lane == 2 * s + v), total, tail)
    packed = jnp.concatenate(
        [
            jnp.concatenate([sums[0:8, :64], sums[8:16, :64]], axis=1),
            jnp.concatenate([sums[16:24, :64], tail], axis=1),
        ],
        axis=0,
    )
    return jnp.concatenate(taps[:32], axis=0), packed


def call(body, out_shapes, *args):
    single = not isinstance(out_shapes, (tuple, list))

    def kernel(*refs):
        ins = [ref[...] for ref in refs[: len(args)]]
        outs = body(*ins)
        for ref, value in zip(refs[len(args) :], [outs] if single else outs):
            ref[...] = value

    return pl.pallas_call(
        kernel,
        out_shape=out_shapes,
        compiler_params=pltpu.CompilerParams(vmem_limit_bytes=40 * 1024 * 1024),
    )(*args)


def sds(shape, dtype):
    return jax.ShapeDtypeStruct(shape, dtype)


def exchange(value, axes):
    return lax.all_to_all(value, axes, split_axis=0, concat_axis=0)


def everyone(value, axes):
    count = math.prod(SIZES[AXES.index(a)] for a in axes)
    return exchange(jnp.broadcast_to(value[None], (count,) + value.shape), axes)


def prepare(vel, cotangent):
    edges = jnp.concatenate([vel[:, :, 0:2], vel[:, :, 254:256]], axis=2).reshape(1, 256)
    return jnp.concatenate(
        [cotangent.astype(BF).reshape(64, 256), edges, jnp.zeros((7, 256), BF)], axis=0
    )


def turns(own, cols):
    ang = TWO_PI / NY * (own * cols % NY).astype(F32)
    return jnp.stack([jnp.cos(ang), jnp.sin(ang)])


def rims_to_send(got, vel, x, yl, w):
    def edges(src):
        return lax.dynamic_index_in_dim(got, src, 0, False)[64].reshape(2, 32, 4)

    def padded(v):
        return jnp.pad(v.reshape(2, 64), ((0, 0), (0, 448)))

    up = padded(edges(jnp.where(yl == 3, (x + 3) % 4, x))[:, :, 2:4])
    down = padded(edges(jnp.where(yl == 0, (x + 1) % 4, x))[:, :, 0:2])
    first, last = vel[:, :2].reshape(2, 512), vel[:, 30:].reshape(2, 512)
    to_y = jnp.arange(4)[:, None, None, None]
    to_w = jnp.arange(WA)[None, :, None, None]
    rows = jnp.where(to_w == (w + 1) % WA, last, first)
    return jnp.where(to_y == yl, rows, jnp.where(to_y == (yl + 1) % 4, up, down))


def velocity_planes(rims, velocity, yl, w):
    def piece(from_y, from_w):
        return lax.dynamic_index_in_dim(rims, (from_y % 4) * WA + from_w % WA, 0, False).astype(F32)

    def side(from_y):
        above, own, below = (piece(from_y, w + d)[:, :64].reshape(2, 32, 2) for d in (31, 0, 1))
        return jnp.concatenate([above[:, 30:], own, below[:, :2]], axis=1)

    mid = jnp.concatenate(
        [piece(yl, w + 31).reshape(2, 2, 256), velocity, piece(yl, w + 1).reshape(2, 2, 256)], axis=1
    )
    full = jnp.concatenate([side(yl + 3), mid, side(yl + 1)], axis=2)
    moved = []
    for s in range(2):
        for b in (-1, 0, 1):
            v = full[s]
            moved.append(
                jnp.concatenate(
                    [v[:, 2 + b : 258 + b], v[:, 1 + b : 2 + b], v[:, 258 + b : 259 + b], jnp.zeros((36, 126), F32)],
                    axis=1,
                )
            )
    moved += [jnp.zeros((36, 384), F32)] * 2
    return jnp.stack(moved, axis=1).reshape(288, 384)


def lift_matrix(lift, kernels):
    parts = []
    for a in range(3):
        for s in range(2):
            for b in range(3):
                parts.append(kernels[:, 3 * a + b] * lift[:, s])
        parts += [jnp.zeros_like(parts[0])] * 2
    return jnp.stack(parts, axis=1)


def finish_velocity(proj, taps, lift, out_w):
    hi = lax.Precision.HIGHEST
    main = proj[:64, :256].reshape(2, 32, 256)
    main_b = main.astype(BF).astype(F32)
    m2 = jnp.dot(lift.T, out_w.astype(F32).T, precision=hi)
    taps = taps.reshape(32, 8, 384)
    out = []
    for s in range(2):
        left, mid, right = taps[:, 3 * s], taps[:, 3 * s + 1], taps[:, 3 * s + 2]
        value = main[s] + m2[s, 0] * main_b[0] + m2[s, 1] * main_b[1] + mid[:, :256]
        value = value + jnp.concatenate([right[:, 256:257], right[:, :255]], axis=1)
        value = value + jnp.concatenate([left[:, 1:256], left[:, 257:258]], axis=1)
        out.append(value)
    return jnp.stack(out)


def finish_weights(total, lift, kernels, point, out_w, lift18):
    hi = lax.Precision.HIGHEST
    scale = 1.0 / math.sqrt(NX * NY)
    total = total * scale
    q = jnp.concatenate([total[:8, :64], total[:8, 64:], total[8:, :64]], axis=0)
    gpt = total[8:10, 64:]
    gpv = total[10, 64:68].reshape(2, 2)
    grad_out = gpt + jnp.dot(gpv, lift.T, precision=hi)
    grad_point = jnp.einsum("ko,ck->oc", q, lift18, precision=hi)
    gv = jnp.einsum("ko,oc->ck", q, point.astype(F32), precision=hi)
    gv = gv.reshape(64, 3, 8)[:, :, :6].reshape(64, 3, 2, 3)
    grad_kernels = jnp.sum(gv * lift[:, None, :, None], axis=2).reshape(64, 9)
    grad_lift = jnp.sum(gv * kernels.reshape(64, 3, 1, 3), axis=(1, 3))
    grad_lift = grad_lift + jnp.dot(out_w.astype(F32).T, gpv, precision=hi)
    return grad_lift, grad_kernels[None], grad_point[None], grad_out


def local(velocity, cotangent, lift_weight, depth_kernels, point_weights, out_weight):
    tab = make_tables()
    x, yl, yh, z, core = (lax.axis_index(a) for a in AXES)
    w = 16 * yh + 2 * z + core
    kernels = depth_kernels[0]
    point = point_weights[0]
    col = jnp.arange(256)[None, :]
    step = jnp.arange(16)[:, None]
    klass = x + 4 * (step // 4)
    turn1 = turns(klass, col + 1024 * (step % 4) + 256 * yl)
    sign = jnp.where(x == 0, (1 - 2 * (col % 2)).astype(F32), 0.0)
    zero = jnp.where(x == 0, jnp.ones((1, 384), F32), 0.0)
    ky_lane = (x + 4 * yl + 16 * (4 * w + jnp.arange(128) // 32)).astype(F32)[None, :]
    cols4 = jnp.asarray(np.concatenate([COL_ID, np.zeros(126, np.int64)]).astype(np.int32))[None, :]
    turn4 = turns(klass, cols4 + 1024 * (step % 4) + 256 * yl + NY)
    lift18 = lift_matrix(lift_weight, kernels)

    vel = velocity.astype(BF)
    got1 = everyone(prepare(vel, cotangent), ("x",))
    spec = call(y_forward, sds((256, 256), BF), got1, turn1, sign, tab["t1"])
    rims = rims_to_send(got1, vel, x, yl, w).reshape(128, 2, 512)
    got2 = exchange(jnp.concatenate([spec.reshape(128, 2, 256), rims], axis=2), ("yl",) + IN_W)
    sent3 = call(
        x_project, sds((64, 384), BF), got2[:, :, :256].reshape(4, 64, 256), ky_lane, tab["d1"], tab["tw1"], tab["kr"], tab["ik"], tab["tw2"], tab["d2"]
    )
    spread = jnp.broadcast_to(sent3.reshape(1, 32, 2, 384), (4, 32, 2, 384)).reshape(128, 2, 384)
    got3 = exchange(spread, ("yl",) + IN_W)
    planes = velocity_planes(got2[:, :, 256:], velocity, yl, w)
    sent4 = call(y_inverse, sds((288, 384), BF), got3.reshape(4, 64, 384), turn4, zero, tab["tk"])
    got4 = exchange(sent4.reshape(4, 72, 384), ("x",))

    def last(got, planes, center, point, lift18, out_cols):
        got = got.astype(F32)
        proj = (got[0] + got[1]) + (got[2] + got[3])
        taps, packed = network(proj, planes, center, point, lift18, out_cols)
        return proj, taps, packed

    proj, taps, packed = call(
        last,
        (sds((72, 384), F32), sds((256, 384), F32), sds((16, 128), F32)),
        got4, planes, velocity.reshape(64, 256), point.astype(F32), lift18, out_weight.astype(F32).T,
    )
    part = jnp.sum(everyone(packed, ("yl", "yh", "c")), axis=0)
    total = jnp.sum(everyone(part, ("x", "z")), axis=0)
    grad_velocity = finish_velocity(proj, taps, lift_weight, out_weight)
    return (grad_velocity,) + finish_weights(total, lift_weight, kernels, point, out_weight, lift18)


def solution(mesh):
    split = jax.sharding.Mesh(mesh.devices.reshape(SIZES), AXES)
    field = P(None, IN_W, IN_H)
    return jax.shard_map(
        local,
        mesh=split,
        in_specs=(field, field, P(), P(), P(), P()),
        out_specs=(field, P(), P(), P(), P()),
        check_vma=False,
    )
```

```python
import math

import jax
import jax.numpy as jnp
import ml_dtypes
import numpy as np
from jax import lax
from jax.experimental import pallas as pl
from jax.experimental.pallas import tpu as pltpu
from jax.sharding import PartitionSpec as P

BF = jnp.bfloat16
F32 = jnp.float32
HA, WA = 16, 32
AXES = ("x", "yl", "yh", "z", "c")
SIZES = (4, 4, 2, 8, 2)
IN_H = ("x", "yl")
IN_W = ("yh", "z", "c")
ROWS, COLS = 32, 256
NX, NY = WA * ROWS, HA * COLS
TWO_PI = 2.0 * math.pi
COL_ID = np.concatenate([np.arange(256), [-1, 256]])


def bf(table):
    return np.asarray(table).astype(ml_dtypes.bfloat16)


def pair(table):
    high = bf(table)
    return np.stack([high, bf(table - high.astype(np.float64))])


def make_tables():
    r = np.arange(256)
    k2 = np.arange(128)
    ang = TWO_PI * (np.outer(k2, r) % 256) / 256
    c, s = np.cos(ang), np.sin(ang)
    t1 = np.stack([np.concatenate([c, s], 1), np.concatenate([-s, c], 1)], 1)
    t1 = t1.reshape(32, 4, 2, 512).transpose(1, 0, 2, 3).reshape(256, 512)

    n32 = np.arange(32)
    a32 = TWO_PI * (np.outer(n32, n32) % 32) / 32
    c32, s32 = np.cos(a32), np.sin(a32)
    d1 = np.zeros((4, 32, 32, 2))
    d1[0, :, :, 0] = c32
    d1[1, :, :, 0] = -s32
    d1[2, :, :, 1] = c32
    d1[3, :, :, 1] = -s32
    d1 = d1.reshape(128, 64)
    tw = TWO_PI * np.outer(n32, np.tile(n32, 8)) / 1024
    tw1 = np.stack([np.cos(tw), np.sin(tw)]).astype(np.float32)

    kr = np.zeros((2, 4, 32, 2, 4, 32))
    ik = np.zeros((2, 4, 32, 2, 256))
    rows = np.concatenate([n32, [-1, 32]])
    a = TWO_PI * np.outer(n32, rows) / 32
    row_of = np.zeros(256)
    for j in range(4):
        kr[0, j, :, 0, j, :] = c32
        kr[1, j, :, 0, j, :] = s32
        kr[1, j, :, 1, j, :] = c32
        kr[0, j, :, 1, j, :] = -s32
        lanes = list(range(j * 32, j * 32 + 32)) + [128 + j * 2, 129 + j * 2]
        row_of[lanes] = rows
        ik[0, j, :, 0, lanes] = np.cos(a).T
        ik[1, j, :, 0, lanes] = -np.sin(a).T
        ik[0, j, :, 1, lanes] = np.sin(a).T
        ik[1, j, :, 1, lanes] = np.cos(a).T
    kr = kr.reshape(256, 256)
    ik = ik.reshape(256, 512)
    tw = TWO_PI * np.outer(n32, row_of) / 1024
    tw2 = np.stack([np.cos(tw), np.sin(tw)]).astype(np.float32)
    d2 = np.zeros((32, 2, 2, 32))
    d2[:, 0, 0] = c32
    d2[:, 0, 1] = -s32
    d2[:, 1, 0] = s32
    d2[:, 1, 1] = c32
    d2 = d2.reshape(64, 64)

    ang = TWO_PI * (np.outer(k2, COL_ID) % 256) / 256
    tk = np.zeros((128, 2, 2, 384))
    tk[:, 0, 0, :258] = 2 * np.cos(ang)
    tk[:, 1, 0, :258] = -2 * np.sin(ang)
    tk[:, 0, 1, :258] = 2 * np.sin(ang)
    tk[:, 1, 1, :258] = 2 * np.cos(ang)
    tk = tk.reshape(32, 4, 2, 768).transpose(1, 0, 2, 3).reshape(256, 768)
    return dict(t1=pair(t1), d1=pair(d1), tw1=tw1, kr=pair(kr), ik=pair(ik), tw2=tw2, d2=pair(d2), tk=bf(tk))


def mm(a, b, ca=1, cb=0):
    return lax.dot_general(a, b, (((ca,), (cb,)), ((), ())), preferred_element_type=F32)


def halves(value):
    high = value.astype(BF)
    return high, (value - high.astype(F32)).astype(BF)


def mm3(a, b, ca=1, cb=0):
    return mm(a[0], b[0], ca, cb) + (mm(a[1], b[0], ca, cb) + mm(a[0], b[1], ca, cb))


def y_forward(got, turn, sign, t1):
    parts = [got[q, :64] for q in range(4)]
    row = lax.broadcasted_iota(jnp.int32, (64, 256), 0)
    pick = jnp.where(row == 1, sign, 0.0).astype(BF)
    result = []
    for e in range(4):
        re = sum(parts[q] * turn[0, 4 * e + q : 4 * e + q + 1] for q in range(4))
        im = -sum(parts[q] * turn[1, 4 * e + q : 4 * e + q + 1] for q in range(4))
        both = halves(jnp.concatenate([re, im], axis=1))
        out = []
        for j in range(4):
            block = mm3((t1[0, j * 64 : (j + 1) * 64], t1[1, j * 64 : (j + 1) * 64]), both, 1, 1)
            if e == 0 and j == 0:
                block = block + mm(pick, both[0][:, :256], 1, 1) + mm(pick, both[1][:, :256], 1, 1)
            out.append(block)
        pieces = [out[j][:, 32 * c : 32 * c + 32] for c in range(2) for j in range(4)]
        result.append(jnp.concatenate(pieces, axis=1))
    return jnp.concatenate(result, axis=0)


def x_project(lines, ky_lane, columns, d1, tw1, kr, ik, tw2, d2):
    first = mm3(d1, halves((lines[0] + lines[1]) + (lines[2] + lines[3])))
    cs, sn = tw1[0], tw1[1]
    turned = []
    for c in range(2):
        for p in range(2):
            re = first[64 * p : 64 * p + 32]
            im = first[64 * p + 32 : 64 * p + 64]
            span = slice(128 * c, 128 * c + 128)
            turned.append(
                jnp.concatenate([(re * cs + im * sn)[:, span], (im * cs - re * sn)[:, span]], axis=1)
            )
    spec = mm3(halves(jnp.concatenate(turned, axis=0)), kr)
    lane = lax.broadcasted_iota(jnp.int32, (32, 128), 1)
    kx = lax.broadcasted_iota(jnp.int32, (32, 128), 0) + 32 * (lane % 32)
    kx = jnp.where(2 * kx >= NX, kx - NX, kx).astype(F32)
    ky = jnp.broadcast_to(ky_lane, (32, 128))
    edge_x = kx == -float(NX // 2)

    def factors(wave_y, edge_y):
        inv = 1.0 / jnp.maximum(kx * kx + wave_y * wave_y, 1.0)
        scale = 1.0 / float(NX * NY)
        cross = jnp.where(edge_x != edge_y, 0.0, -kx * wave_y * inv)
        return (1.0 - kx * kx * inv) * scale, cross * scale, (1.0 - wave_y * wave_y * inv) * scale

    ar, br, dr = factors(ky, jnp.zeros((32, 128), jnp.bool_))
    packed = ky == 0.0
    ai, bi, di = factors(jnp.where(packed, -float(NY // 2), ky), packed)
    (r0, r0i), (i0, i0i), (r1, r1i), (i1, i1i) = (
        (spec[32 * i : 32 * i + 32, :128], spec[32 * i : 32 * i + 32, 128:]) for i in range(4)
    )
    first = jnp.concatenate(
        [ar * r0 + br * r1 - (ai * i0i + bi * i1i), ar * r0i + br * r1i + ai * i0 + bi * i1], axis=1
    )
    second = jnp.concatenate(
        [br * r0 + dr * r1 - (bi * i0i + di * i1i), br * r0i + dr * r1i + bi * i0 + di * i1], axis=1
    )
    back = mm3(halves(jnp.concatenate([first, second], axis=0)), ik)
    cs, sn = tw2[0], tw2[1]
    main, rim = [], []
    for c in range(2):
        re = back[32 * c : 32 * c + 32, :256]
        im = back[32 * c : 32 * c + 32, 256:]
        value = jnp.concatenate([re * cs - im * sn, re * sn + im * cs], axis=0)
        main.append(value[:, :128])
        rim.append(value[:, 128:136])
    stack = jnp.concatenate(main + rim + [jnp.zeros((64, 112), F32)], axis=1)
    out = mm3(d2, halves(stack))
    even = lax.broadcasted_iota(jnp.int32, (64, 384), 0) % 2 == 0
    return jnp.concatenate(
        [(out + jnp.where(even, columns[2 * y : 2 * y + 1], columns[2 * y + 1 : 2 * y + 2])).astype(BF) for y in range(4)],
        axis=0,
    )


def regroup(lines):
    a = lax.broadcasted_iota(jnp.int32, (64, 64), 0)
    b = lax.broadcasted_iota(jnp.int32, (64, 64), 1)
    eye = jnp.where(a == b, 1.0, 0.0).astype(BF)
    turned = mm(lines, eye, 0, 0)
    main = jnp.concatenate(
        [
            jnp.concatenate([turned[32 * j : 32 * j + 32] for j in range(4)], axis=1),
            jnp.concatenate([turned[128 + 32 * j : 160 + 32 * j] for j in range(4)], axis=1),
        ],
        axis=0,
    )
    rim = jnp.concatenate(
        [jnp.concatenate([turned[256 + 8 * c + 2 * j : 258 + 8 * c + 2 * j] for j in range(4)], axis=1) for c in range(2)],
        axis=0,
    )
    return jnp.concatenate([main, rim, jnp.zeros((4, 256), F32)], axis=0).astype(BF)


def y_inverse(got, turn, zero, tk):
    lane = lax.broadcasted_iota(jnp.int32, (1, 384), 1)
    odd = jnp.where(lane < 256, lane % 2, (lane == 256).astype(jnp.int32)).astype(F32)
    acc = [None] * 4
    for e in range(4):
        lines = regroup(got[e])
        part = mm(lines, tk)
        re, im = part[:, :384], part[:, 384:]
        if e == 0:
            own = lines.astype(F32)
            once = zero * (own[:, 1:2] * (1.0 - 2.0 * odd) - own[:, 0:1])
        for d in range(4):
            i = 4 * e + d
            piece = re * turn[0, i : i + 1] - im * turn[1, i : i + 1]
            acc[d] = piece + once if e == 0 else acc[d] + piece
    return jnp.concatenate(acc, axis=0)


def network(proj, planes, center, point, lift18, out_cols):
    mix = lax.dot_general(point, lift18, (((1,), (0,)), ((), ())), precision=lax.Precision.HIGHEST, preferred_element_type=F32)
    mix_hi, mix_lo = halves(mix)
    mix3 = jnp.concatenate([mix_hi, mix_lo, mix_hi], axis=1)
    mix2 = mix3[:, :48]
    mix4 = jnp.concatenate([mix2, mix2], axis=0)
    taps = [None] * 34
    sums = jnp.zeros((56, 128), F32)
    for i in range(-1, 33):
        view, view_lo = halves(planes[(i + 1) * 8 : (i + 4) * 8])
        t = jnp.tanh(mm(mix3, jnp.concatenate([view, view, view_lo], axis=0)))
        ids = (64, 66) if i < 0 else (65, 67) if i >= 32 else (i, 32 + i)
        g0 = proj[ids[0] : ids[0] + 1]
        g1 = proj[ids[1] : ids[1] + 1]
        grad = out_cols[:, 0:1] * g0 + out_cols[:, 1:2] * g1
        gz, gz_lo = halves(grad * (1.0 - t * t))
        tap = mm(mix4, jnp.concatenate([gz, gz_lo], axis=0), 0, 0)
        tap = tap[:24] + tap[24:]
        for a in range(3):
            k = i + a - 1
            if 0 <= k < 32:
                piece = tap[a * 8 : a * 8 + 8]
                taps[k] = piece if taps[k] is None else taps[k] + piece
        if 0 <= i < 32:
            g = jnp.concatenate([g0[:, :256], g1[:, :256]], axis=0)
            g_hi, g_lo = halves(g)
            g8 = jnp.concatenate([g_hi.astype(F32), g_lo.astype(F32), jnp.zeros((4, 256), F32)], axis=0).astype(BF)
            left = jnp.concatenate([view[:, :256], view_lo[:, :256], g8], axis=0)
            t_hi, t_lo = halves(t[:, :256])
            sums = sums + (
                mm(left, jnp.concatenate([gz[:, :256], t_hi], axis=0), 1, 1)
                + mm(left, jnp.concatenate([gz_lo[:, :256], t_lo], axis=0), 1, 1)
            )
    tail = sums[48:50, 64:] + sums[50:52, 64:]
    tail = jnp.concatenate([tail, jnp.zeros((6, 64), F32)], axis=0)
    sums = sums[:24] + sums[24:48]
    row = lax.broadcasted_iota(jnp.int32, (8, 64), 0)
    lane = lax.broadcasted_iota(jnp.int32, (8, 64), 1)
    for s in range(2):
        for v in range(2):
            prod = proj[32 * s : 32 * s + 32, :256] * center[32 * v : 32 * v + 32]
            total = jnp.sum(jnp.sum(prod, axis=0, keepdims=True), axis=1, keepdims=True)
            tail = jnp.where((row == 2) & (lane == 2 * s + v), total, tail)
    packed = jnp.concatenate(
        [
            jnp.concatenate([sums[0:8, :64], sums[8:16, :64]], axis=1),
            jnp.concatenate([sums[16:24, :64], tail], axis=1),
        ],
        axis=0,
    )
    return jnp.concatenate(taps[:32], axis=0), jnp.concatenate([packed] * 16, axis=0)


def call(body, out_shapes, *args):
    single = not isinstance(out_shapes, (tuple, list))

    def kernel(*refs):
        ins = [ref[...] for ref in refs[: len(args)]]
        outs = body(*ins)
        for ref, value in zip(refs[len(args) :], [outs] if single else outs):
            ref[...] = value

    return pl.pallas_call(
        kernel,
        out_shape=out_shapes,
        compiler_params=pltpu.CompilerParams(vmem_limit_bytes=40 * 1024 * 1024),
    )(*args)


def sds(shape, dtype):
    return jax.ShapeDtypeStruct(shape, dtype)


def exchange(value, axes):
    return lax.all_to_all(value, axes, split_axis=0, concat_axis=0)


def from_row_neighbour(value, step):
    return lax.ppermute(value, IN_W, [(i, (i + step) % WA) for i in range(WA)])


def pack_first(vel, cotangent):
    edges = jnp.concatenate([vel[:, 0:2], vel[:, 254:256], jnp.zeros((64, 124), F32)], axis=1).T[:8]
    rows = jnp.concatenate([edges, jnp.zeros((8, 192), F32)], axis=1)
    return jnp.concatenate([cotangent, rows] * 4, axis=0)


def sum_and_spread(got):
    total = got[0]
    for i in range(1, 16):
        total = total + got[i]
    return jnp.concatenate([total] * 32, axis=0)


def turns(own, cols):
    ang = TWO_PI / NY * (own * cols % NY).astype(F32)
    return jnp.stack([jnp.cos(ang), jnp.sin(ang)])


def columns_to_send(got, x, yl):
    def edges(src, first):
        rows = lax.dynamic_index_in_dim(got, src, 0, False)
        return rows[64 + first : 66 + first, :64]

    up = edges(jnp.where(yl == 3, (x + 3) % 4, x), 2)
    down = edges(jnp.where(yl == 0, (x + 1) % 4, x), 0)
    to_y = jnp.arange(4)[:, None, None]
    cols = jnp.where(to_y == (yl + 1) % 4, up, down)
    return jnp.pad(cols.reshape(8, 64), ((0, 0), (272, 48)))


def velocity_planes(columns, above, velocity, below, yl, w):
    def side(from_y):
        def piece(from_w):
            v = lax.dynamic_index_in_dim(columns, (from_y % 4) * WA + from_w % WA, 0, False)
            return v.astype(F32).reshape(2, 2, 32).transpose(1, 2, 0)

        return jnp.concatenate([piece(w + 31)[:, 30:], piece(w), piece(w + 1)[:, :2]], axis=1)

    mid = jnp.concatenate([above, velocity, below], axis=1)
    full = jnp.concatenate([side(yl + 3), mid, side(yl + 1)], axis=2)
    moved = []
    for s in range(2):
        for b in (-1, 0, 1):
            v = full[s]
            moved.append(
                jnp.concatenate(
                    [v[:, 2 + b : 258 + b], v[:, 1 + b : 2 + b], v[:, 258 + b : 259 + b], jnp.zeros((36, 126), F32)],
                    axis=1,
                )
            )
    moved += [jnp.zeros((36, 384), F32)] * 2
    return jnp.stack(moved, axis=1).reshape(288, 384)


def lift_matrix(lift, kernels):
    parts = []
    for a in range(3):
        for s in range(2):
            for b in range(3):
                parts.append(kernels[:, 3 * a + b] * lift[:, s])
        parts += [jnp.zeros_like(parts[0])] * 2
    return jnp.stack(parts, axis=1)


def finish_velocity(proj, taps, lift, out_w):
    hi = lax.Precision.HIGHEST
    main = proj[:64, :256].reshape(2, 32, 256)
    m2 = jnp.dot(lift.T, out_w.astype(F32).T, precision=hi)
    taps = taps.reshape(32, 8, 384)
    out = []
    for s in range(2):
        left, mid, right = taps[:, 3 * s], taps[:, 3 * s + 1], taps[:, 3 * s + 2]
        value = main[s] + m2[s, 0] * main[0] + m2[s, 1] * main[1] + mid[:, :256]
        value = value + jnp.concatenate([right[:, 256:257], right[:, :255]], axis=1)
        value = value + jnp.concatenate([left[:, 1:256], left[:, 257:258]], axis=1)
        out.append(value)
    return jnp.stack(out)


def finish_weights(got, lift, lift_rows, kernels, point, out_cols, lift18_rows):
    hi = lax.Precision.HIGHEST
    total = got[0]
    for i in range(1, 32):
        total = total + got[i]
    total = total * (1.0 / math.sqrt(NX * NY))
    q = jnp.concatenate([total[:8, :64], total[:8, 64:], total[8:, :64]], axis=0)

    def pair_sum(s, v):
        return total[10:11, 64 + 2 * s + v : 65 + 2 * s + v]

    grad_out = [
        total[8 + s : 9 + s, 64:] + pair_sum(s, 0) * lift_rows[0:1] + pair_sum(s, 1) * lift_rows[1:2] for s in range(2)
    ]
    grad_point = lax.dot_general(q, lift18_rows, (((0,), (0,)), ((), ())), precision=hi, preferred_element_type=F32)
    gv = lax.dot_general(point, q, (((0,), (1,)), ((), ())), precision=hi, preferred_element_type=F32)
    grad_kernels = [
        lift[:, 0:1] * gv[:, 8 * a : 8 * a + 3] + lift[:, 1:2] * gv[:, 8 * a + 3 : 8 * a + 6] for a in range(3)
    ]
    grad_lift = []
    for s in range(2):
        value = out_cols[:, 0:1] * pair_sum(0, s) + out_cols[:, 1:2] * pair_sum(1, s)
        for a in range(3):
            first = 8 * a + 3 * s
            value = value + jnp.sum(kernels[:, 3 * a : 3 * a + 3] * gv[:, first : first + 3], axis=1, keepdims=True)
        grad_lift.append(value)
    return (
        jnp.concatenate(grad_lift, axis=1),
        jnp.concatenate(grad_kernels, axis=1),
        grad_point,
        jnp.concatenate(grad_out, axis=0),
    )


def local(velocity, cotangent, lift_weight, depth_kernels, point_weights, out_weight):
    tab = make_tables()
    x, yl, yh, z, core = (lax.axis_index(a) for a in AXES)
    w = 16 * yh + 2 * z + core
    kernels = depth_kernels[0]
    point = point_weights[0]
    col = jnp.arange(256)[None, :]
    step = jnp.arange(16)[:, None]
    klass = x + 4 * (step // 4)
    turn1 = turns(klass, col + 1024 * (step % 4) + 256 * yl)
    sign = jnp.where(x == 0, (1 - 2 * (col % 2)).astype(F32), 0.0)
    zero = jnp.where(x == 0, jnp.ones((1, 384), F32), 0.0)
    ky_lane = (x + 4 * yl + 16 * (4 * w + jnp.arange(128) // 32)).astype(F32)[None, :]
    cols4 = jnp.asarray(np.concatenate([COL_ID, np.zeros(126, np.int64)]).astype(np.int32))[None, :]
    turn4 = turns(klass, cols4 + 1024 * (step % 4) + 256 * yl + NY)
    lift18 = lift_matrix(lift_weight, kernels)

    above = from_row_neighbour(velocity[:, 30:], 1)
    below = from_row_neighbour(velocity[:, :2], -1)
    sent1 = call(pack_first, sds((288, 256), F32), velocity.reshape(64, 256), cotangent.reshape(64, 256))
    got1 = exchange(sent1.reshape(4, 72, 256), ("x",))
    spec = call(y_forward, sds((256, 256), F32), got1, turn1, sign, tab["t1"])
    got2 = exchange(spec.reshape(128, 2, 256), ("yl",) + IN_W)
    columns = columns_to_send(got1, x, yl)
    sent3 = call(
        x_project, sds((256, 384), BF), got2.reshape(4, 64, 256), ky_lane, columns, tab["d1"], tab["tw1"], tab["kr"], tab["ik"], tab["tw2"], tab["d2"]
    )
    got3 = exchange(sent3.reshape(128, 2, 384), ("yl",) + IN_W)
    planes = velocity_planes(got3[:, :, 272:336], above, velocity, below, yl, w)
    sent4 = call(y_inverse, sds((288, 384), F32), got3.reshape(4, 64, 384), turn4, zero, tab["tk"])
    got4 = exchange(sent4.reshape(4, 72, 384), ("x",))

    def last(got, planes, center, point, lift18, out_cols):
        proj = (got[0] + got[1]) + (got[2] + got[3])
        taps, packed = network(proj, planes, center, point, lift18, out_cols)
        return proj, taps, packed

    point_f = point.astype(F32)
    out_cols = out_weight.astype(F32).T
    proj, taps, packed = call(
        last,
        (sds((72, 384), F32), sds((256, 384), F32), sds((256, 128), F32)),
        got4, planes, velocity.reshape(64, 256), point_f, lift18, out_cols,
    )
    part = exchange(packed.reshape(16, 16, 128), ("yl", "yh", "c"))
    part = call(sum_and_spread, sds((512, 128), F32), part)
    total = exchange(part.reshape(32, 16, 128), ("x", "z"))
    grad_velocity = finish_velocity(proj, taps, lift_weight, out_weight)
    grad_lift, grad_kernels, grad_point, grad_out = call(
        finish_weights,
        (sds((64, 2), F32), sds((64, 9), F32), sds((64, 64), F32), sds((2, 64), F32)),
        total, lift_weight, lift_weight.T, kernels, point_f, out_cols, lift18.T,
    )
    return grad_velocity, grad_lift, grad_kernels[None], grad_point[None], grad_out


def solution(mesh):
    split = jax.sharding.Mesh(mesh.devices.reshape(SIZES), AXES)
    field = P(None, IN_W, IN_H)
    return jax.shard_map(
        local,
        mesh=split,
        in_specs=(field, field, P(), P(), P(), P()),
        out_specs=(field, P(), P(), P(), P()),
        check_vma=False,
    )
```

```python
import math

import jax
import jax.numpy as jnp
import ml_dtypes
import numpy as np
from jax import lax
from jax.experimental import pallas as pl
from jax.experimental.pallas import tpu as pltpu
from jax.sharding import PartitionSpec as P

BF = jnp.bfloat16
F32 = jnp.float32
HA, WA = 16, 32
AXES = ("x", "yl", "yh", "z", "c")
SIZES = (4, 4, 2, 8, 2)
IN_H = ("x", "yl")
IN_W = ("yh", "z", "c")
ROWS, COLS = 32, 256
NX, NY = WA * ROWS, HA * COLS
TWO_PI = 2.0 * math.pi
COL_ID = np.concatenate([np.arange(256), [-1, 256]])


def bf(table):
    return np.asarray(table).astype(ml_dtypes.bfloat16)


def pair(table):
    high = bf(table)
    return np.stack([high, bf(table - high.astype(np.float64))])


def make_tables():
    r = np.arange(256)
    k2 = np.arange(128)
    ang = TWO_PI * (np.outer(k2, r) % 256) / 256
    c, s = np.cos(ang), np.sin(ang)
    t1 = np.stack([np.concatenate([c, s], 1), np.concatenate([-s, c], 1)], 1)
    t1 = t1.reshape(32, 4, 2, 512).transpose(1, 0, 2, 3).reshape(256, 512)

    n32 = np.arange(32)
    a32 = TWO_PI * (np.outer(n32, n32) % 32) / 32
    c32, s32 = np.cos(a32), np.sin(a32)
    d1 = np.zeros((4, 32, 32, 2))
    d1[0, :, :, 0] = c32
    d1[1, :, :, 0] = -s32
    d1[2, :, :, 1] = c32
    d1[3, :, :, 1] = -s32
    d1 = d1.reshape(128, 64)
    tw = TWO_PI * np.outer(n32, np.tile(n32, 8)) / 1024
    tw1 = np.stack([np.cos(tw), np.sin(tw)]).astype(np.float32)

    kr = np.zeros((2, 4, 32, 2, 4, 32))
    ik = np.zeros((2, 4, 32, 2, 256))
    rows = np.concatenate([n32, [-1, 32]])
    a = TWO_PI * np.outer(n32, rows) / 32
    row_of = np.zeros(256)
    for j in range(4):
        kr[0, j, :, 0, j, :] = c32
        kr[1, j, :, 0, j, :] = s32
        kr[1, j, :, 1, j, :] = c32
        kr[0, j, :, 1, j, :] = -s32
        lanes = list(range(j * 32, j * 32 + 32)) + [128 + j * 2, 129 + j * 2]
        row_of[lanes] = rows
        ik[0, j, :, 0, lanes] = np.cos(a).T
        ik[1, j, :, 0, lanes] = -np.sin(a).T
        ik[0, j, :, 1, lanes] = np.sin(a).T
        ik[1, j, :, 1, lanes] = np.cos(a).T
    kr = kr.reshape(256, 256)
    ik = ik.reshape(256, 512)
    tw = TWO_PI * np.outer(n32, row_of) / 1024
    tw2 = np.stack([np.cos(tw), np.sin(tw)]).astype(np.float32)
    d2 = np.zeros((32, 2, 2, 32))
    d2[:, 0, 0] = c32
    d2[:, 0, 1] = -s32
    d2[:, 1, 0] = s32
    d2[:, 1, 1] = c32
    d2 = d2.reshape(64, 64)

    ang = TWO_PI * (np.outer(k2, COL_ID) % 256) / 256
    tk = np.zeros((128, 2, 2, 384))
    tk[:, 0, 0, :258] = 2 * np.cos(ang)
    tk[:, 1, 0, :258] = -2 * np.sin(ang)
    tk[:, 0, 1, :258] = 2 * np.sin(ang)
    tk[:, 1, 1, :258] = 2 * np.cos(ang)
    tk = tk.reshape(32, 4, 2, 768).transpose(1, 0, 2, 3).reshape(256, 768)
    return dict(t1=pair(t1), d1=pair(d1), tw1=tw1, kr=pair(kr), ik=pair(ik), tw2=tw2, d2=pair(d2), tk=bf(tk))


def mm(a, b, ca=1, cb=0):
    return lax.dot_general(a, b, (((ca,), (cb,)), ((), ())), preferred_element_type=F32)


def halves(value):
    high = value.astype(BF)
    return high, (value - high.astype(F32)).astype(BF)


def mm3(a, b, ca=1, cb=0):
    return mm(a[0], b[0], ca, cb) + (mm(a[1], b[0], ca, cb) + mm(a[0], b[1], ca, cb))


def y_forward(got, turn, sign, t1):
    parts = [got[q, :64] for q in range(4)]
    row = lax.broadcasted_iota(jnp.int32, (64, 256), 0)
    pick = jnp.where(row == 1, sign, 0.0).astype(BF)
    result = []
    for e in range(4):
        re = sum(parts[q] * turn[0, 4 * e + q : 4 * e + q + 1] for q in range(4))
        im = -sum(parts[q] * turn[1, 4 * e + q : 4 * e + q + 1] for q in range(4))
        both = halves(jnp.concatenate([re, im], axis=1))
        out = []
        for j in range(4):
            block = mm3((t1[0, j * 64 : (j + 1) * 64], t1[1, j * 64 : (j + 1) * 64]), both, 1, 1)
            if e == 0 and j == 0:
                block = block + mm(pick, both[0][:, :256], 1, 1) + mm(pick, both[1][:, :256], 1, 1)
            out.append(block)
        pieces = [out[j][:, 32 * c : 32 * c + 32] for c in range(2) for j in range(4)]
        result.append(jnp.concatenate(pieces, axis=1))
    return jnp.concatenate(result, axis=0).reshape(128, 2, 256)


def x_project(lines, ky_lane, columns, d1, tw1, kr, ik, tw2, d2):
    first = mm3(d1, halves((lines[0] + lines[1]) + (lines[2] + lines[3])))
    cs, sn = tw1[0], tw1[1]
    turned = []
    for c in range(2):
        for p in range(2):
            re = first[64 * p : 64 * p + 32]
            im = first[64 * p + 32 : 64 * p + 64]
            span = slice(128 * c, 128 * c + 128)
            turned.append(
                jnp.concatenate([(re * cs + im * sn)[:, span], (im * cs - re * sn)[:, span]], axis=1)
            )
    spec = mm3(halves(jnp.concatenate(turned, axis=0)), kr)
    lane = lax.broadcasted_iota(jnp.int32, (32, 128), 1)
    kx = lax.broadcasted_iota(jnp.int32, (32, 128), 0) + 32 * (lane % 32)
    kx = jnp.where(2 * kx >= NX, kx - NX, kx).astype(F32)
    ky = jnp.broadcast_to(ky_lane, (32, 128))
    edge_x = kx == -float(NX // 2)

    def factors(wave_y, edge_y):
        inv = 1.0 / jnp.maximum(kx * kx + wave_y * wave_y, 1.0)
        scale = 1.0 / float(NX * NY)
        cross = jnp.where(edge_x != edge_y, 0.0, -kx * wave_y * inv)
        return (1.0 - kx * kx * inv) * scale, cross * scale, (1.0 - wave_y * wave_y * inv) * scale

    ar, br, dr = factors(ky, jnp.zeros((32, 128), jnp.bool_))
    packed = ky == 0.0
    ai, bi, di = factors(jnp.where(packed, -float(NY // 2), ky), packed)
    (r0, r0i), (i0, i0i), (r1, r1i), (i1, i1i) = (
        (spec[32 * i : 32 * i + 32, :128], spec[32 * i : 32 * i + 32, 128:]) for i in range(4)
    )
    first = jnp.concatenate(
        [ar * r0 + br * r1 - (ai * i0i + bi * i1i), ar * r0i + br * r1i + ai * i0 + bi * i1], axis=1
    )
    second = jnp.concatenate(
        [br * r0 + dr * r1 - (bi * i0i + di * i1i), br * r0i + dr * r1i + bi * i0 + di * i1], axis=1
    )
    back = mm3(halves(jnp.concatenate([first, second], axis=0)), ik)
    cs, sn = tw2[0], tw2[1]
    main, rim = [], []
    for c in range(2):
        re = back[32 * c : 32 * c + 32, :256]
        im = back[32 * c : 32 * c + 32, 256:]
        value = jnp.concatenate([re * cs - im * sn, re * sn + im * cs], axis=0)
        main.append(value[:, :128])
        rim.append(value[:, 128:136])
    stack = jnp.concatenate(main + rim + [jnp.zeros((64, 112), F32)], axis=1)
    out = mm3(d2, halves(stack))
    even = lax.broadcasted_iota(jnp.int32, (64, 384), 0) % 2 == 0
    return jnp.concatenate(
        [(out + jnp.where(even, columns[2 * y : 2 * y + 1], columns[2 * y + 1 : 2 * y + 2])).astype(BF) for y in range(4)],
        axis=0,
    )


def regroup(lines):
    a = lax.broadcasted_iota(jnp.int32, (64, 64), 0)
    b = lax.broadcasted_iota(jnp.int32, (64, 64), 1)
    eye = jnp.where(a == b, 1.0, 0.0).astype(BF)
    turned = mm(lines, eye, 0, 0)
    main = jnp.concatenate(
        [
            jnp.concatenate([turned[32 * j : 32 * j + 32] for j in range(4)], axis=1),
            jnp.concatenate([turned[128 + 32 * j : 160 + 32 * j] for j in range(4)], axis=1),
        ],
        axis=0,
    )
    rim = jnp.concatenate(
        [jnp.concatenate([turned[256 + 8 * c + 2 * j : 258 + 8 * c + 2 * j] for j in range(4)], axis=1) for c in range(2)],
        axis=0,
    )
    return jnp.concatenate([main, rim, jnp.zeros((4, 256), F32)], axis=0).astype(BF)


def y_inverse(got, turn, zero, tk):
    lane = lax.broadcasted_iota(jnp.int32, (1, 384), 1)
    odd = jnp.where(lane < 256, lane % 2, (lane == 256).astype(jnp.int32)).astype(F32)
    acc = [None] * 4
    for e in range(4):
        lines = regroup(got[e])
        part = mm(lines, tk)
        re, im = part[:, :384], part[:, 384:]
        if e == 0:
            own = lines.astype(F32)
            once = zero * (own[:, 1:2] * (1.0 - 2.0 * odd) - own[:, 0:1])
        for d in range(4):
            i = 4 * e + d
            piece = re * turn[0, i : i + 1] - im * turn[1, i : i + 1]
            acc[d] = piece + once if e == 0 else acc[d] + piece
    return jnp.concatenate(acc, axis=0)


def network(proj, planes, center, point, lift18, out_cols):
    mix = lax.dot_general(point, lift18, (((1,), (0,)), ((), ())), precision=lax.Precision.HIGHEST, preferred_element_type=F32)
    mix_hi, mix_lo = halves(mix)
    mix3 = jnp.concatenate([mix_hi, mix_lo, mix_hi], axis=1)
    mix2 = mix3[:, :48]
    mix4 = jnp.concatenate([mix2, mix2], axis=0)
    taps = [None] * 34
    sums = jnp.zeros((56, 128), F32)
    for i in range(-1, 33):
        view, view_lo = halves(planes[(i + 1) * 8 : (i + 4) * 8])
        t = jnp.tanh(mm(mix3, jnp.concatenate([view, view, view_lo], axis=0)))
        ids = (64, 66) if i < 0 else (65, 67) if i >= 32 else (i, 32 + i)
        g0 = proj[ids[0] : ids[0] + 1]
        g1 = proj[ids[1] : ids[1] + 1]
        grad = out_cols[:, 0:1] * g0 + out_cols[:, 1:2] * g1
        gz, gz_lo = halves(grad * (1.0 - t * t))
        tap = mm(mix4, jnp.concatenate([gz, gz_lo], axis=0), 0, 0)
        tap = tap[:24] + tap[24:]
        for a in range(3):
            k = i + a - 1
            if 0 <= k < 32:
                piece = tap[a * 8 : a * 8 + 8]
                taps[k] = piece if taps[k] is None else taps[k] + piece
        if 0 <= i < 32:
            g = jnp.concatenate([g0[:, :256], g1[:, :256]], axis=0)
            g_hi, g_lo = halves(g)
            g8 = jnp.concatenate([g_hi.astype(F32), g_lo.astype(F32), jnp.zeros((4, 256), F32)], axis=0).astype(BF)
            left = jnp.concatenate([view[:, :256], view_lo[:, :256], g8], axis=0)
            t_hi, t_lo = halves(t[:, :256])
            sums = sums + (
                mm(left, jnp.concatenate([gz[:, :256], t_hi], axis=0), 1, 1)
                + mm(left, jnp.concatenate([gz_lo[:, :256], t_lo], axis=0), 1, 1)
            )
    tail = sums[48:50, 64:] + sums[50:52, 64:]
    tail = jnp.concatenate([tail, jnp.zeros((6, 64), F32)], axis=0)
    sums = sums[:24] + sums[24:48]
    row = lax.broadcasted_iota(jnp.int32, (8, 64), 0)
    lane = lax.broadcasted_iota(jnp.int32, (8, 64), 1)
    for s in range(2):
        for v in range(2):
            prod = proj[32 * s : 32 * s + 32, :256] * center[32 * v : 32 * v + 32]
            total = jnp.sum(jnp.sum(prod, axis=0, keepdims=True), axis=1, keepdims=True)
            tail = jnp.where((row == 2) & (lane == 2 * s + v), total, tail)
    packed = jnp.concatenate(
        [
            jnp.concatenate([sums[0:8, :64], sums[8:16, :64]], axis=1),
            jnp.concatenate([sums[16:24, :64], tail], axis=1),
        ],
        axis=0,
    )
    return jnp.concatenate(taps[:32], axis=0), jnp.concatenate([packed] * 16, axis=0)


def call(body, out_shapes, *args):
    single = not isinstance(out_shapes, (tuple, list))

    def kernel(*refs):
        ins = [ref[...] for ref in refs[: len(args)]]
        outs = body(*ins)
        for ref, value in zip(refs[len(args) :], [outs] if single else outs):
            ref[...] = value

    return pl.pallas_call(
        kernel,
        out_shape=out_shapes,
        compiler_params=pltpu.CompilerParams(vmem_limit_bytes=40 * 1024 * 1024),
    )(*args)


def sds(shape, dtype):
    return jax.ShapeDtypeStruct(shape, dtype)


def exchange(value, axes):
    return lax.all_to_all(value, axes, split_axis=0, concat_axis=0)


def from_row_neighbour(value, step):
    return lax.ppermute(value, IN_W, [(i, (i + step) % WA) for i in range(WA)])


def pack_first(vel, cotangent):
    edges = jnp.concatenate([vel[:, 0:2], vel[:, 254:256], jnp.zeros((64, 124), F32)], axis=1).T[:8]
    rows = jnp.concatenate([edges, jnp.zeros((8, 192), F32)], axis=1)
    return jnp.concatenate([cotangent, rows] * 4, axis=0)


def sum_and_spread(got):
    total = got[0]
    for i in range(1, 16):
        total = total + got[i]
    return jnp.concatenate([total] * 32, axis=0)


def turns(own, cols):
    ang = TWO_PI / NY * (own * cols % NY).astype(F32)
    return jnp.stack([jnp.cos(ang), jnp.sin(ang)])


def columns_to_send(got, x, yl):
    def edges(src, first):
        rows = lax.dynamic_index_in_dim(got, src, 0, False)
        return rows[64 + first : 66 + first, :64]

    up = edges(jnp.where(yl == 3, (x + 3) % 4, x), 2)
    down = edges(jnp.where(yl == 0, (x + 1) % 4, x), 0)
    to_y = jnp.arange(4)[:, None, None]
    cols = jnp.where(to_y == (yl + 1) % 4, up, down)
    return jnp.pad(cols.reshape(8, 64), ((0, 0), (272, 48)))


def velocity_planes(columns, above, velocity, below, yl, w):
    def side(from_y):
        def piece(from_w):
            v = lax.dynamic_index_in_dim(columns, (from_y % 4) * WA + from_w % WA, 0, False)
            return v.astype(F32).reshape(2, 2, 32).transpose(1, 2, 0)

        return jnp.concatenate([piece(w + 31)[:, 30:], piece(w), piece(w + 1)[:, :2]], axis=1)

    mid = jnp.concatenate([above, velocity, below], axis=1)
    full = jnp.concatenate([side(yl + 3), mid, side(yl + 1)], axis=2)
    moved = []
    for s in range(2):
        for b in (-1, 0, 1):
            v = full[s]
            moved.append(
                jnp.concatenate(
                    [v[:, 2 + b : 258 + b], v[:, 1 + b : 2 + b], v[:, 258 + b : 259 + b], jnp.zeros((36, 126), F32)],
                    axis=1,
                )
            )
    moved += [jnp.zeros((36, 384), F32)] * 2
    return jnp.stack(moved, axis=1).reshape(288, 384)


def lift_matrix(lift, kernels):
    parts = []
    for a in range(3):
        for s in range(2):
            for b in range(3):
                parts.append(kernels[:, 3 * a + b] * lift[:, s])
        parts += [jnp.zeros_like(parts[0])] * 2
    return jnp.stack(parts, axis=1)


def finish_velocity(proj, taps, lift, out_w):
    hi = lax.Precision.HIGHEST
    main = proj[:64, :256].reshape(2, 32, 256)
    m2 = jnp.dot(lift.T, out_w.astype(F32).T, precision=hi)
    taps = taps.reshape(32, 8, 384)
    out = []
    for s in range(2):
        left, mid, right = taps[:, 3 * s], taps[:, 3 * s + 1], taps[:, 3 * s + 2]
        value = main[s] + m2[s, 0] * main[0] + m2[s, 1] * main[1] + mid[:, :256]
        value = value + jnp.concatenate([right[:, 256:257], right[:, :255]], axis=1)
        value = value + jnp.concatenate([left[:, 1:256], left[:, 257:258]], axis=1)
        out.append(value)
    return jnp.stack(out)


def finish_weights(got, lift_rows, kernel_rows, point, out_rows, lift18_rows):
    hi = lax.Precision.HIGHEST
    total = got[0]
    for i in range(1, 32):
        total = total + got[i]
    total = total * (1.0 / math.sqrt(NX * NY))
    q = jnp.concatenate([total[:8, :64], total[:8, 64:], total[8:, :64]], axis=0)

    def pair_sum(s, v):
        return total[10:11, 64 + 2 * s + v : 65 + 2 * s + v]

    grad_out = [
        total[8 + s : 9 + s, 64:] + pair_sum(s, 0) * lift_rows[0:1] + pair_sum(s, 1) * lift_rows[1:2] for s in range(2)
    ]
    grad_point = lax.dot_general(q, lift18_rows, (((0,), (0,)), ((), ())), precision=hi, preferred_element_type=F32)
    gv = lax.dot_general(q, point, (((1,), (0,)), ((), ())), precision=hi, preferred_element_type=F32)
    grad_kernels = [
        lift_rows[0:1] * gv[8 * a : 8 * a + 3] + lift_rows[1:2] * gv[8 * a + 3 : 8 * a + 6] for a in range(3)
    ]
    grad_lift = []
    for s in range(2):
        value = out_rows[0:1] * pair_sum(0, s) + out_rows[1:2] * pair_sum(1, s)
        for a in range(3):
            first = 8 * a + 3 * s
            value = value + jnp.sum(kernel_rows[3 * a : 3 * a + 3] * gv[first : first + 3], axis=0, keepdims=True)
        grad_lift.append(value)
    return (
        jnp.concatenate(grad_lift, axis=0),
        jnp.concatenate(grad_kernels, axis=0).reshape(9, 1, 64),
        grad_point,
        jnp.concatenate(grad_out, axis=0),
    )


def local(velocity, cotangent, lift_weight, depth_kernels, point_weights, out_weight):
    tab = make_tables()
    x, yl, yh, z, core = (lax.axis_index(a) for a in AXES)
    w = 16 * yh + 2 * z + core
    kernels = depth_kernels[0]
    point = point_weights[0]
    col = jnp.arange(256)[None, :]
    step = jnp.arange(16)[:, None]
    klass = x + 4 * (step // 4)
    turn1 = turns(klass, col + 1024 * (step % 4) + 256 * yl)
    sign = jnp.where(x == 0, (1 - 2 * (col % 2)).astype(F32), 0.0)
    zero = jnp.where(x == 0, jnp.ones((1, 384), F32), 0.0)
    ky_lane = (x + 4 * yl + 16 * (4 * w + jnp.arange(128) // 32)).astype(F32)[None, :]
    cols4 = jnp.asarray(np.concatenate([COL_ID, np.zeros(126, np.int64)]).astype(np.int32))[None, :]
    turn4 = turns(klass, cols4 + 1024 * (step % 4) + 256 * yl + NY)
    lift18 = lift_matrix(lift_weight, kernels)

    sent1 = call(pack_first, sds((288, 256), F32), velocity.reshape(64, 256), cotangent.reshape(64, 256))
    got1 = exchange(sent1.reshape(4, 72, 256), ("x",))
    spec = call(y_forward, sds((128, 2, 256), F32), got1, turn1, sign, tab["t1"])
    spec, bottom, top = lax.optimization_barrier((spec, velocity[:, 30:], velocity[:, :2]))
    got2 = exchange(spec, ("yl",) + IN_W)
    above = from_row_neighbour(bottom, 1)
    below = from_row_neighbour(top, -1)
    columns = columns_to_send(got1, x, yl)
    sent3 = call(
        x_project, sds((256, 384), BF), got2.reshape(4, 64, 256), ky_lane, columns, tab["d1"], tab["tw1"], tab["kr"], tab["ik"], tab["tw2"], tab["d2"]
    )
    got3 = exchange(sent3.reshape(128, 2, 384), ("yl",) + IN_W)
    sent4 = call(y_inverse, sds((288, 384), F32), got3.reshape(4, 64, 384), turn4, zero, tab["tk"])
    sent4, got3 = lax.optimization_barrier((sent4, got3))
    got4 = exchange(sent4.reshape(4, 72, 384), ("x",))
    planes = velocity_planes(got3[:, :, 272:336], above, velocity, below, yl, w)

    def last(got, planes, center, point, lift18, out_cols):
        proj = (got[0] + got[1]) + (got[2] + got[3])
        taps, packed = network(proj, planes, center, point, lift18, out_cols)
        return proj, taps, packed

    point_f = point.astype(F32)
    out_cols = out_weight.astype(F32).T
    proj, taps, packed = call(
        last,
        (sds((72, 384), F32), sds((256, 384), F32), sds((256, 128), F32)),
        got4, planes, velocity.reshape(64, 256), point_f, lift18, out_cols,
    )
    part = exchange(packed.reshape(16, 16, 128), ("yl", "yh", "c"))
    part = call(sum_and_spread, sds((512, 128), F32), part)
    total = exchange(part.reshape(32, 16, 128), ("x", "z"))
    grad_velocity = finish_velocity(proj, taps, lift_weight, out_weight)
    grad_lift, grad_kernels, grad_point, grad_out = call(
        finish_weights,
        (sds((2, 64), F32), sds((9, 1, 64), F32), sds((64, 64), F32), sds((2, 64), F32)),
        total, lift_weight.T, kernels.T, point_f, out_weight.astype(F32), lift18.T,
    )
    return grad_velocity, grad_lift.T, grad_kernels.transpose(1, 2, 0), grad_point[None], grad_out


def solution(mesh):
    split = jax.sharding.Mesh(mesh.devices.reshape(SIZES), AXES)
    field = P(None, IN_W, IN_H)
    return jax.shard_map(
        local,
        mesh=split,
        in_specs=(field, field, P(), P(), P(), P()),
        out_specs=(field, P(), P(), P(), P()),
        check_vma=False,
    )
```

```python
import math

import jax
import jax.numpy as jnp
import ml_dtypes
import numpy as np
from jax import lax
from jax.experimental import pallas as pl
from jax.experimental.pallas import tpu as pltpu
from jax.sharding import PartitionSpec as P

BF = jnp.bfloat16
F32 = jnp.float32
HA, WA = 16, 32
AXES = ("x", "yl", "yh", "z", "c")
SIZES = (4, 4, 2, 8, 2)
IN_H = ("x", "yl")
IN_W = ("yh", "z", "c")
ROWS, COLS = 32, 256
NX, NY = WA * ROWS, HA * COLS
TWO_PI = 2.0 * math.pi
COL_ID = np.concatenate([np.arange(257), np.zeros(126, np.int64), [-1]])
COL_USED = np.concatenate([np.ones(257), np.zeros(126), [1]])


def bf(table):
    return np.asarray(table).astype(ml_dtypes.bfloat16)


def pair(table):
    high = bf(table)
    return np.stack([high, bf(table - high.astype(np.float64))])


def make_tables():
    r = np.arange(256)
    k2 = np.arange(128)
    ang = TWO_PI * (np.outer(k2, r) % 256) / 256
    c, s = np.cos(ang), np.sin(ang)
    t1 = np.stack([np.concatenate([c, s], 1), np.concatenate([-s, c], 1)], 1)
    t1 = t1.reshape(32, 4, 2, 512).transpose(1, 0, 2, 3).reshape(256, 512)

    n32 = np.arange(32)
    a32 = TWO_PI * (np.outer(n32, n32) % 32) / 32
    c32, s32 = np.cos(a32), np.sin(a32)
    d1 = np.zeros((4, 32, 32, 2))
    d1[0, :, :, 0] = c32
    d1[1, :, :, 0] = -s32
    d1[2, :, :, 1] = c32
    d1[3, :, :, 1] = -s32
    d1 = d1.reshape(128, 64)
    tw = TWO_PI * np.outer(n32, np.tile(n32, 8)) / 1024
    tw1 = np.stack([np.cos(tw), np.sin(tw)]).astype(np.float32)

    kr = np.zeros((2, 4, 32, 2, 4, 32))
    ik = np.zeros((2, 4, 32, 2, 256))
    rows = np.concatenate([n32, [-1, 32]])
    a = TWO_PI * np.outer(n32, rows) / 32
    row_of = np.zeros(256)
    for j in range(4):
        kr[0, j, :, 0, j, :] = c32
        kr[1, j, :, 0, j, :] = s32
        kr[1, j, :, 1, j, :] = c32
        kr[0, j, :, 1, j, :] = -s32
        lanes = list(range(j * 32, j * 32 + 32)) + [128 + j * 2, 129 + j * 2]
        row_of[lanes] = rows
        ik[0, j, :, 0, lanes] = np.cos(a).T
        ik[1, j, :, 0, lanes] = -np.sin(a).T
        ik[0, j, :, 1, lanes] = np.sin(a).T
        ik[1, j, :, 1, lanes] = np.cos(a).T
    kr = kr.reshape(256, 256)
    ik = ik.reshape(256, 512)
    tw = TWO_PI * np.outer(n32, row_of) / 1024
    tw2 = np.stack([np.cos(tw), np.sin(tw)]).astype(np.float32)
    d2 = np.zeros((32, 2, 2, 32))
    d2[:, 0, 0] = c32
    d2[:, 0, 1] = -s32
    d2[:, 1, 0] = s32
    d2[:, 1, 1] = c32
    d2 = d2.reshape(64, 64)

    ang = TWO_PI * (np.outer(k2, COL_ID) % 256) / 256
    tk = np.zeros((128, 2, 2, 384))
    tk[:, 0, 0] = 2 * np.cos(ang) * COL_USED
    tk[:, 1, 0] = -2 * np.sin(ang) * COL_USED
    tk[:, 0, 1] = 2 * np.sin(ang) * COL_USED
    tk[:, 1, 1] = 2 * np.cos(ang) * COL_USED
    tk = tk.reshape(32, 4, 2, 768).transpose(1, 0, 2, 3).reshape(256, 768)
    return dict(t1=pair(t1), d1=pair(d1), tw1=tw1, kr=pair(kr), ik=pair(ik), tw2=tw2, d2=pair(d2), tk=bf(tk))


def mm(a, b, ca=1, cb=0):
    return lax.dot_general(a, b, (((ca,), (cb,)), ((), ())), preferred_element_type=F32)


def halves(value):
    high = value.astype(BF)
    return high, (value - high.astype(F32)).astype(BF)


def mm3(a, b, ca=1, cb=0):
    return mm(a[0], b[0], ca, cb) + (mm(a[1], b[0], ca, cb) + mm(a[0], b[1], ca, cb))


def y_forward(got, turn, sign, t1):
    parts = [got[q, :64] for q in range(4)]
    row = lax.broadcasted_iota(jnp.int32, (64, 256), 0)
    pick = jnp.where(row == 1, sign, 0.0).astype(BF)
    result = []
    for e in range(4):
        re = sum(parts[q] * turn[0, 4 * e + q : 4 * e + q + 1] for q in range(4))
        im = -sum(parts[q] * turn[1, 4 * e + q : 4 * e + q + 1] for q in range(4))
        both = halves(jnp.concatenate([re, im], axis=1))
        out = []
        for j in range(4):
            block = mm3((t1[0, j * 64 : (j + 1) * 64], t1[1, j * 64 : (j + 1) * 64]), both, 1, 1)
            if e == 0 and j == 0:
                block = block + mm(pick, both[0][:, :256], 1, 1) + mm(pick, both[1][:, :256], 1, 1)
            out.append(block)
        pieces = [out[j][:, 32 * c : 32 * c + 32] for c in range(2) for j in range(4)]
        result.append(jnp.concatenate(pieces, axis=1))
    return jnp.concatenate(result, axis=0).reshape(128, 2, 256)


def x_project(lines, ky_lane, columns, d1, tw1, kr, ik, tw2, d2):
    first = mm3(d1, halves((lines[0] + lines[1]) + (lines[2] + lines[3])))
    cs, sn = tw1[0], tw1[1]
    turned = []
    for c in range(2):
        for p in range(2):
            re = first[64 * p : 64 * p + 32]
            im = first[64 * p + 32 : 64 * p + 64]
            span = slice(128 * c, 128 * c + 128)
            turned.append(
                jnp.concatenate([(re * cs + im * sn)[:, span], (im * cs - re * sn)[:, span]], axis=1)
            )
    spec = mm3(halves(jnp.concatenate(turned, axis=0)), kr)
    lane = lax.broadcasted_iota(jnp.int32, (32, 128), 1)
    kx = lax.broadcasted_iota(jnp.int32, (32, 128), 0) + 32 * (lane % 32)
    kx = jnp.where(2 * kx >= NX, kx - NX, kx).astype(F32)
    ky = jnp.broadcast_to(ky_lane, (32, 128))
    edge_x = kx == -float(NX // 2)

    def factors(wave_y, edge_y):
        inv = 1.0 / jnp.maximum(kx * kx + wave_y * wave_y, 1.0)
        scale = 1.0 / float(NX * NY)
        cross = jnp.where(edge_x != edge_y, 0.0, -kx * wave_y * inv)
        return (1.0 - kx * kx * inv) * scale, cross * scale, (1.0 - wave_y * wave_y * inv) * scale

    ar, br, dr = factors(ky, jnp.zeros((32, 128), jnp.bool_))
    packed = ky == 0.0
    ai, bi, di = factors(jnp.where(packed, -float(NY // 2), ky), packed)
    (r0, r0i), (i0, i0i), (r1, r1i), (i1, i1i) = (
        (spec[32 * i : 32 * i + 32, :128], spec[32 * i : 32 * i + 32, 128:]) for i in range(4)
    )
    first = jnp.concatenate(
        [ar * r0 + br * r1 - (ai * i0i + bi * i1i), ar * r0i + br * r1i + ai * i0 + bi * i1], axis=1
    )
    second = jnp.concatenate(
        [br * r0 + dr * r1 - (bi * i0i + di * i1i), br * r0i + dr * r1i + bi * i0 + di * i1], axis=1
    )
    back = mm3(halves(jnp.concatenate([first, second], axis=0)), ik)
    cs, sn = tw2[0], tw2[1]
    main, rim = [], []
    for c in range(2):
        re = back[32 * c : 32 * c + 32, :256]
        im = back[32 * c : 32 * c + 32, 256:]
        value = jnp.concatenate([re * cs - im * sn, re * sn + im * cs], axis=0)
        main.append(value[:, :128])
        rim.append(value[:, 128:136])
    stack = jnp.concatenate(main + rim + [jnp.zeros((64, 112), F32)], axis=1)
    out = mm3(d2, halves(stack))
    even = lax.broadcasted_iota(jnp.int32, (64, 384), 0) % 2 == 0
    return jnp.concatenate(
        [(out + jnp.where(even, columns[2 * y : 2 * y + 1], columns[2 * y + 1 : 2 * y + 2])).astype(BF) for y in range(4)],
        axis=0,
    )


def regroup(lines):
    a = lax.broadcasted_iota(jnp.int32, (64, 64), 0)
    b = lax.broadcasted_iota(jnp.int32, (64, 64), 1)
    eye = jnp.where(a == b, 1.0, 0.0).astype(BF)
    turned = mm(lines, eye, 0, 0)
    main = jnp.concatenate(
        [
            jnp.concatenate([turned[32 * j : 32 * j + 32] for j in range(4)], axis=1),
            jnp.concatenate([turned[128 + 32 * j : 160 + 32 * j] for j in range(4)], axis=1),
        ],
        axis=0,
    )
    rim = jnp.concatenate(
        [jnp.concatenate([turned[256 + 8 * c + 2 * j : 258 + 8 * c + 2 * j] for j in range(4)], axis=1) for c in range(2)],
        axis=0,
    )
    return jnp.concatenate([main, rim, jnp.zeros((4, 256), F32)], axis=0).astype(BF)


def y_inverse(got, turn, zero, tk):
    lane = lax.broadcasted_iota(jnp.int32, (1, 384), 1)
    odd = (lane % 2).astype(F32)
    acc = [None] * 4
    for e in range(4):
        lines = regroup(got[e])
        part = mm(lines, tk)
        re, im = part[:, :384], part[:, 384:]
        if e == 0:
            own = lines.astype(F32)
            once = zero * (own[:, 1:2] * (1.0 - 2.0 * odd) - own[:, 0:1])
        for d in range(4):
            i = 4 * e + d
            piece = re * turn[0, i : i + 1] - im * turn[1, i : i + 1]
            acc[d] = piece + once if e == 0 else acc[d] + piece
    return jnp.concatenate(acc, axis=0)


def activations(pieces, above, center, below, point, lift18):
    mix = lax.dot_general(point, lift18, (((1,), (0,)), ((), ())), precision=lax.Precision.HIGHEST, preferred_element_type=F32)
    mix_hi, mix_lo = halves(mix)
    mix3 = jnp.concatenate([mix_hi, mix_lo, mix_hi], axis=1)
    a = lax.broadcasted_iota(jnp.int32, (64, 64), 0)
    b = lax.broadcasted_iota(jnp.int32, (64, 64), 1)
    eye = jnp.where(a == b, 1.0, 0.0).astype(BF)
    lines = jnp.concatenate([p.astype(F32)[:, 272:336] for p in pieces] + [jnp.zeros((4, 64), F32)], axis=0)
    turned = mm(eye, lines.astype(BF), 1, 1)
    moved = []
    for s in range(2):
        rows = turned[32 * s : 32 * s + 32]

        def side(k):
            return jnp.concatenate(
                [rows[30:, 2 * k : 2 * k + 2], rows[:, 2 * k + 2 : 2 * k + 4], rows[:2, 2 * k + 4 : 2 * k + 6]], axis=0
            )

        mid = jnp.concatenate([above[s], center[32 * s : 32 * s + 32], below[s]], axis=0)
        full = jnp.concatenate([mid, side(3), jnp.zeros((36, 124), F32), side(0)], axis=1)
        moved.append(jnp.concatenate([full[:, 383:], full[:, :383]], axis=1))
        moved.append(full)
        moved.append(jnp.concatenate([full[:, 1:], full[:, :1]], axis=1))
    blocks = [
        jnp.concatenate([m[r : r + 1] for m in moved] + [jnp.zeros((2, 384), F32)], axis=0) for r in range(36)
    ]
    result = []
    for i in range(34):
        view, view_lo = halves(jnp.concatenate(blocks[i : i + 3], axis=0))
        result.append(jnp.tanh(mm(mix3, jnp.concatenate([view, view, view_lo], axis=0))).astype(BF))
    mix2 = mix3[:, :48]
    return jnp.concatenate(blocks, axis=0), jnp.concatenate(result, axis=0), jnp.concatenate([mix2, mix2], axis=0)


def network(proj, planes, squash, mix4, center, out_cols):
    taps = [None] * 34
    sums = jnp.zeros((56, 128), F32)
    rest = jnp.zeros((56, 64), F32)
    for i in range(-1, 33):
        t_b = squash[(i + 1) * 64 : (i + 2) * 64]
        t = t_b.astype(F32)
        ids = (64, 66) if i < 0 else (65, 67) if i >= 32 else (i, 32 + i)
        g0 = proj[ids[0] : ids[0] + 1]
        g1 = proj[ids[1] : ids[1] + 1]
        grad = out_cols[:, 0:1] * g0 + out_cols[:, 1:2] * g1
        gz, gz_lo = halves(grad * (1.0 - t * t))
        tap = mm(mix4, jnp.concatenate([gz, gz_lo], axis=0), 0, 0)
        tap = tap[:24] + tap[24:]
        for a in range(3):
            k = i + a - 1
            if 0 <= k < 32:
                piece = tap[a * 8 : a * 8 + 8]
                taps[k] = piece if taps[k] is None else taps[k] + piece
        if 0 <= i < 32:
            view, view_lo = halves(planes[(i + 1) * 8 : (i + 4) * 8, :256])
            g_hi, g_lo = halves(jnp.concatenate([g0[:, :256], g1[:, :256]], axis=0))
            g8 = jnp.concatenate([g_hi.astype(F32), g_lo.astype(F32), jnp.zeros((4, 256), F32)], axis=0).astype(BF)
            left = jnp.concatenate([view, view_lo, g8], axis=0)
            sums = sums + mm(left, jnp.concatenate([gz[:, :256], t_b[:, :256]], axis=0), 1, 1)
            rest = rest + mm(left, gz_lo[:, :256], 1, 1)
    tail = sums[48:50, 64:] + sums[50:52, 64:]
    tail = jnp.concatenate([tail, jnp.zeros((6, 64), F32)], axis=0)
    sums = sums[:24, :64] + sums[24:48, :64] + (rest[:24] + rest[24:48])
    row = lax.broadcasted_iota(jnp.int32, (8, 64), 0)
    lane = lax.broadcasted_iota(jnp.int32, (8, 64), 1)
    for s in range(2):
        for v in range(2):
            prod = proj[32 * s : 32 * s + 32, :256] * center[32 * v : 32 * v + 32]
            total = jnp.sum(jnp.sum(prod, axis=0, keepdims=True), axis=1, keepdims=True)
            tail = jnp.where((row == 2) & (lane == 2 * s + v), total, tail)
    packed = jnp.concatenate(
        [
            jnp.concatenate([sums[0:8], sums[8:16]], axis=1),
            jnp.concatenate([sums[16:24], tail], axis=1),
        ],
        axis=0,
    )
    return jnp.concatenate(taps[:32], axis=0), jnp.concatenate([packed] * 16, axis=0)


def call(body, out_shapes, *args):
    single = not isinstance(out_shapes, (tuple, list))

    def kernel(*refs):
        ins = [ref[...] for ref in refs[: len(args)]]
        outs = body(*ins)
        for ref, value in zip(refs[len(args) :], [outs] if single else outs):
            ref[...] = value

    return pl.pallas_call(
        kernel,
        out_shape=out_shapes,
        compiler_params=pltpu.CompilerParams(vmem_limit_bytes=40 * 1024 * 1024),
    )(*args)


def call_picked(body, out_shapes, index, picked, *args):
    def kernel(index_ref, picked_ref, *refs):
        pieces = [picked_ref[index_ref[k]] for k in range(index.shape[0])]
        outs = body(pieces, *[ref[...] for ref in refs[: len(args)]])
        for ref, value in zip(refs[len(args) :], outs):
            ref[...] = value

    vmem = pl.BlockSpec(memory_space=pltpu.VMEM)
    return pl.pallas_call(
        kernel,
        in_specs=[pl.BlockSpec(memory_space=pltpu.SMEM)] + [vmem] * (1 + len(args)),
        out_specs=[vmem] * len(out_shapes),
        out_shape=out_shapes,
        compiler_params=pltpu.CompilerParams(vmem_limit_bytes=40 * 1024 * 1024),
    )(index, picked, *args)


def sds(shape, dtype):
    return jax.ShapeDtypeStruct(shape, dtype)


def exchange(value, axes):
    return lax.all_to_all(value, axes, split_axis=0, concat_axis=0)


def from_row_neighbour(value, step):
    return lax.ppermute(value, IN_W, [(i, (i + step) % WA) for i in range(WA)])


def pack_first(vel, cotangent):
    edges = jnp.concatenate([vel[:, 0:2], vel[:, 254:256], jnp.zeros((64, 124), F32)], axis=1).T[:8]
    rows = jnp.concatenate([edges, jnp.zeros((8, 192), F32)], axis=1)
    return jnp.concatenate([cotangent, rows] * 4, axis=0)


def sum_and_spread(got):
    total = got[0]
    for i in range(1, 16):
        total = total + got[i]
    return jnp.concatenate([total] * 32, axis=0)


def turns(own, cols):
    ang = TWO_PI / NY * (own * cols % NY).astype(F32)
    return jnp.stack([jnp.cos(ang), jnp.sin(ang)])


def columns_to_send(got, x, yl):
    def edges(src, first):
        rows = lax.dynamic_index_in_dim(got, src, 0, False)
        return rows[64 + first : 66 + first, :64]

    up = edges(jnp.where(yl == 3, (x + 3) % 4, x), 2)
    down = edges(jnp.where(yl == 0, (x + 1) % 4, x), 0)
    to_y = jnp.arange(4)[:, None, None]
    cols = jnp.where(to_y == (yl + 1) % 4, up, down)
    return jnp.pad(cols.reshape(8, 64), ((0, 0), (272, 48)))


def lift_matrix(lift, kernels):
    parts = []
    for a in range(3):
        for s in range(2):
            for b in range(3):
                parts.append(kernels[:, 3 * a + b] * lift[:, s])
        parts += [jnp.zeros_like(parts[0])] * 2
    return jnp.stack(parts, axis=1)


def finish_velocity(proj, taps, lift, out_w):
    hi = lax.Precision.HIGHEST
    main = proj[:64, :256].reshape(2, 32, 256)
    m2 = jnp.dot(lift.T, out_w.astype(F32).T, precision=hi)
    taps = taps.reshape(32, 8, 384)
    out = []
    for s in range(2):
        left, mid, right = taps[:, 3 * s], taps[:, 3 * s + 1], taps[:, 3 * s + 2]
        value = main[s] + m2[s, 0] * main[0] + m2[s, 1] * main[1] + mid[:, :256]
        value = value + jnp.concatenate([right[:, 383:], right[:, :255]], axis=1)
        value = value + left[:, 1:257]
        out.append(value)
    return jnp.stack(out)


def finish_weights(got, lift_rows, kernel_rows, point, out_rows, lift18_rows):
    hi = lax.Precision.HIGHEST
    total = got[0]
    for i in range(1, 32):
        total = total + got[i]
    total = total * (1.0 / math.sqrt(NX * NY))
    q = jnp.concatenate([total[:8, :64], total[:8, 64:], total[8:, :64]], axis=0)

    def pair_sum(s, v):
        return total[10:11, 64 + 2 * s + v : 65 + 2 * s + v]

    grad_out = [
        total[8 + s : 9 + s, 64:] + pair_sum(s, 0) * lift_rows[0:1] + pair_sum(s, 1) * lift_rows[1:2] for s in range(2)
    ]
    grad_point = lax.dot_general(q, lift18_rows, (((0,), (0,)), ((), ())), precision=hi, preferred_element_type=F32)
    gv = lax.dot_general(q, point, (((1,), (0,)), ((), ())), precision=hi, preferred_element_type=F32)
    grad_kernels = [
        lift_rows[0:1] * gv[8 * a : 8 * a + 3] + lift_rows[1:2] * gv[8 * a + 3 : 8 * a + 6] for a in range(3)
    ]
    grad_lift = []
    for s in range(2):
        value = out_rows[0:1] * pair_sum(0, s) + out_rows[1:2] * pair_sum(1, s)
        for a in range(3):
            first = 8 * a + 3 * s
            value = value + jnp.sum(kernel_rows[3 * a : 3 * a + 3] * gv[first : first + 3], axis=0, keepdims=True)
        grad_lift.append(value)
    return (
        jnp.concatenate(grad_lift, axis=0),
        jnp.concatenate(grad_kernels, axis=0).reshape(9, 1, 64),
        grad_point,
        jnp.concatenate(grad_out, axis=0),
    )


def local(velocity, cotangent, lift_weight, depth_kernels, point_weights, out_weight):
    tab = make_tables()
    x, yl, yh, z, core = (lax.axis_index(a) for a in AXES)
    w = 16 * yh + 2 * z + core
    kernels = depth_kernels[0]
    point = point_weights[0]
    col = jnp.arange(256)[None, :]
    step = jnp.arange(16)[:, None]
    klass = x + 4 * (step // 4)
    turn1 = turns(klass, col + 1024 * (step % 4) + 256 * yl)
    sign = jnp.where(x == 0, (1 - 2 * (col % 2)).astype(F32), 0.0)
    zero = jnp.where(x == 0, jnp.ones((1, 384), F32), 0.0)
    ky_lane = (x + 4 * yl + 16 * (4 * w + jnp.arange(128) // 32)).astype(F32)[None, :]
    cols4 = jnp.asarray(COL_ID.astype(np.int32))[None, :]
    turn4 = turns(klass, cols4 + 1024 * (step % 4) + 256 * yl + NY)
    lift18 = lift_matrix(lift_weight, kernels)

    sent1 = call(pack_first, sds((288, 256), F32), velocity.reshape(64, 256), cotangent.reshape(64, 256))
    got1 = exchange(sent1.reshape(4, 72, 256), ("x",))
    spec = call(y_forward, sds((128, 2, 256), F32), got1, turn1, sign, tab["t1"])
    spec, bottom, top = lax.optimization_barrier((spec, velocity[:, 30:], velocity[:, :2]))
    got2 = exchange(spec, ("yl",) + IN_W)
    above = from_row_neighbour(bottom, 1)
    below = from_row_neighbour(top, -1)
    columns = columns_to_send(got1, x, yl)
    sent3 = call(
        x_project, sds((256, 384), BF), got2.reshape(4, 64, 256), ky_lane, columns, tab["d1"], tab["tw1"], tab["kr"], tab["ik"], tab["tw2"], tab["d2"]
    )
    sent3, above, below = lax.optimization_barrier((sent3, above, below))
    got3 = exchange(sent3.reshape(128, 2, 384), ("yl",) + IN_W)
    sent4 = call(y_inverse, sds((288, 384), F32), got3.reshape(4, 64, 384), turn4, zero, tab["tk"])
    got4 = exchange(sent4.reshape(4, 72, 384), ("x",))
    point_f = point.astype(F32)
    out_cols = out_weight.astype(F32).T
    center = velocity.reshape(64, 256)
    near = [((yl + dy) % 4) * WA + (w + dw) % WA for dy in (3, 1) for dw in (31, 0, 1)]
    planes, squash, mix4 = call_picked(
        activations,
        (sds((288, 384), F32), sds((34 * 64, 384), BF), sds((128, 48), BF)),
        jnp.stack(near).astype(jnp.int32), got3, above, center, below, point_f, lift18,
    )

    def last(got, *rest):
        proj = (got[0] + got[1]) + (got[2] + got[3])
        return (proj,) + network(proj, *rest)

    proj, taps, packed = call(
        last,
        (sds((72, 384), F32), sds((256, 384), F32), sds((256, 128), F32)),
        got4, planes, squash, mix4, center, out_cols,
    )
    part = exchange(packed.reshape(16, 16, 128), ("yl", "yh", "c"))
    part = call(sum_and_spread, sds((512, 128), F32), part)
    total = exchange(part.reshape(32, 16, 128), ("x", "z"))
    grad_velocity = finish_velocity(proj, taps, lift_weight, out_weight)
    grad_lift, grad_kernels, grad_point, grad_out = call(
        finish_weights,
        (sds((2, 64), F32), sds((9, 1, 64), F32), sds((64, 64), F32), sds((2, 64), F32)),
        total, lift_weight.T, kernels.T, point_f, out_weight.astype(F32), lift18.T,
    )
    return grad_velocity, grad_lift.T, grad_kernels.transpose(1, 2, 0), grad_point[None], grad_out


def solution(mesh):
    split = jax.sharding.Mesh(mesh.devices.reshape(SIZES), AXES)
    field = P(None, IN_W, IN_H)
    return jax.shard_map(
        local,
        mesh=split,
        in_specs=(field, field, P(), P(), P(), P()),
        out_specs=(field, P(), P(), P(), P()),
        check_vma=False,
    )
```

```python
import math

import jax
import jax.numpy as jnp
import ml_dtypes
import numpy as np
from jax import lax
from jax.experimental import pallas as pl
from jax.experimental.pallas import tpu as pltpu
from jax.sharding import PartitionSpec as P

BF = jnp.bfloat16
F32 = jnp.float32
HA, WA = 16, 32
AXES = ("x", "yl", "yh", "z", "c")
SIZES = (4, 4, 2, 8, 2)
IN_H = ("x", "yl")
IN_W = ("yh", "z", "c")
ROWS, COLS = 32, 256
NX, NY = WA * ROWS, HA * COLS
TWO_PI = 2.0 * math.pi
COL_ID = np.concatenate([np.arange(257), np.zeros(126, np.int64), [-1]])
COL_USED = np.concatenate([np.ones(257), np.zeros(126), [1]])


def bf(table):
    return np.asarray(table).astype(ml_dtypes.bfloat16)


def pair(table):
    high = bf(table)
    return np.stack([high, bf(table - high.astype(np.float64))])


def make_tables():
    r = np.arange(256)
    k2 = np.arange(128)
    ang = TWO_PI * (np.outer(k2, r) % 256) / 256
    c, s = np.cos(ang), np.sin(ang)
    t1 = np.stack([np.concatenate([c, s], 1), np.concatenate([-s, c], 1)], 1)
    t1 = t1.reshape(32, 4, 2, 512).transpose(1, 0, 2, 3).reshape(256, 512)

    n32 = np.arange(32)
    a32 = TWO_PI * (np.outer(n32, n32) % 32) / 32
    c32, s32 = np.cos(a32), np.sin(a32)
    d1 = np.zeros((4, 32, 32, 2))
    d1[0, :, :, 0] = c32
    d1[1, :, :, 0] = -s32
    d1[2, :, :, 1] = c32
    d1[3, :, :, 1] = -s32
    d1 = d1.reshape(128, 64)
    tw = TWO_PI * np.outer(n32, np.tile(n32, 8)) / 1024
    tw1 = np.stack([np.cos(tw), np.sin(tw)]).astype(np.float32)

    kr = np.zeros((2, 4, 32, 2, 4, 32))
    ik = np.zeros((2, 4, 32, 2, 256))
    rows = np.concatenate([n32, [-1, 32]])
    a = TWO_PI * np.outer(n32, rows) / 32
    row_of = np.zeros(256)
    for j in range(4):
        kr[0, j, :, 0, j, :] = c32
        kr[1, j, :, 0, j, :] = s32
        kr[1, j, :, 1, j, :] = c32
        kr[0, j, :, 1, j, :] = -s32
        lanes = list(range(j * 32, j * 32 + 32)) + [128 + j * 2, 129 + j * 2]
        row_of[lanes] = rows
        ik[0, j, :, 0, lanes] = np.cos(a).T
        ik[1, j, :, 0, lanes] = -np.sin(a).T
        ik[0, j, :, 1, lanes] = np.sin(a).T
        ik[1, j, :, 1, lanes] = np.cos(a).T
    kr = kr.reshape(256, 256)
    ik = ik.reshape(256, 512)
    tw = TWO_PI * np.outer(n32, row_of) / 1024
    tw2 = np.stack([np.cos(tw), np.sin(tw)]).astype(np.float32)
    d2 = np.zeros((32, 2, 2, 32))
    d2[:, 0, 0] = c32
    d2[:, 0, 1] = -s32
    d2[:, 1, 0] = s32
    d2[:, 1, 1] = c32
    d2 = d2.reshape(64, 64)

    ang = TWO_PI * (np.outer(k2, COL_ID) % 256) / 256
    tk = np.zeros((128, 2, 2, 384))
    tk[:, 0, 0] = 2 * np.cos(ang) * COL_USED
    tk[:, 1, 0] = -2 * np.sin(ang) * COL_USED
    tk[:, 0, 1] = 2 * np.sin(ang) * COL_USED
    tk[:, 1, 1] = 2 * np.cos(ang) * COL_USED
    tk = tk.reshape(32, 4, 2, 768).transpose(1, 0, 2, 3).reshape(256, 768)
    return dict(t1=pair(t1), d1=pair(d1), tw1=tw1, kr=pair(kr), ik=pair(ik), tw2=tw2, d2=pair(d2), tk=bf(tk))


def mm(a, b, ca=1, cb=0):
    return lax.dot_general(a, b, (((ca,), (cb,)), ((), ())), preferred_element_type=F32)


def halves(value):
    high = value.astype(BF)
    return high, (value - high.astype(F32)).astype(BF)


def mm3(a, b, ca=1, cb=0):
    return mm(a[0], b[0], ca, cb) + (mm(a[1], b[0], ca, cb) + mm(a[0], b[1], ca, cb))


def y_forward(got, turn, sign, t1):
    parts = [got[q, :64] for q in range(4)]
    row = lax.broadcasted_iota(jnp.int32, (64, 256), 0)
    pick = jnp.where(row == 1, sign, 0.0).astype(BF)
    result = []
    for e in range(4):
        re = sum(parts[q] * turn[0, 4 * e + q : 4 * e + q + 1] for q in range(4))
        im = -sum(parts[q] * turn[1, 4 * e + q : 4 * e + q + 1] for q in range(4))
        both = halves(jnp.concatenate([re, im], axis=1))
        out = []
        for j in range(4):
            block = mm3((t1[0, j * 64 : (j + 1) * 64], t1[1, j * 64 : (j + 1) * 64]), both, 1, 1)
            if e == 0 and j == 0:
                block = block + mm(pick, both[0][:, :256], 1, 1) + mm(pick, both[1][:, :256], 1, 1)
            out.append(block)
        pieces = [out[j][:, 32 * c : 32 * c + 32] for c in range(2) for j in range(4)]
        result.append(jnp.concatenate(pieces, axis=1))
    return jnp.concatenate(result, axis=0).reshape(128, 2, 256)


def x_project(lines, ky_lane, columns, d1, tw1, kr, ik, tw2, d2):
    first = mm3(d1, halves((lines[0] + lines[1]) + (lines[2] + lines[3])))
    cs, sn = tw1[0], tw1[1]
    turned = []
    for c in range(2):
        for p in range(2):
            re = first[64 * p : 64 * p + 32]
            im = first[64 * p + 32 : 64 * p + 64]
            span = slice(128 * c, 128 * c + 128)
            turned.append(
                jnp.concatenate([(re * cs + im * sn)[:, span], (im * cs - re * sn)[:, span]], axis=1)
            )
    spec = mm3(halves(jnp.concatenate(turned, axis=0)), kr)
    lane = lax.broadcasted_iota(jnp.int32, (32, 128), 1)
    kx = lax.broadcasted_iota(jnp.int32, (32, 128), 0) + 32 * (lane % 32)
    kx = jnp.where(2 * kx >= NX, kx - NX, kx).astype(F32)
    ky = jnp.broadcast_to(ky_lane, (32, 128))
    edge_x = kx == -float(NX // 2)

    def factors(wave_y, edge_y):
        inv = 1.0 / jnp.maximum(kx * kx + wave_y * wave_y, 1.0)
        scale = 1.0 / float(NX * NY)
        cross = jnp.where(edge_x != edge_y, 0.0, -kx * wave_y * inv)
        return (1.0 - kx * kx * inv) * scale, cross * scale, (1.0 - wave_y * wave_y * inv) * scale

    ar, br, dr = factors(ky, jnp.zeros((32, 128), jnp.bool_))
    packed = ky == 0.0
    ai, bi, di = factors(jnp.where(packed, -float(NY // 2), ky), packed)
    (r0, r0i), (i0, i0i), (r1, r1i), (i1, i1i) = (
        (spec[32 * i : 32 * i + 32, :128], spec[32 * i : 32 * i + 32, 128:]) for i in range(4)
    )
    first = jnp.concatenate(
        [ar * r0 + br * r1 - (ai * i0i + bi * i1i), ar * r0i + br * r1i + ai * i0 + bi * i1], axis=1
    )
    second = jnp.concatenate(
        [br * r0 + dr * r1 - (bi * i0i + di * i1i), br * r0i + dr * r1i + bi * i0 + di * i1], axis=1
    )
    back = mm3(halves(jnp.concatenate([first, second], axis=0)), ik)
    cs, sn = tw2[0], tw2[1]
    main, rim = [], []
    for c in range(2):
        re = back[32 * c : 32 * c + 32, :256]
        im = back[32 * c : 32 * c + 32, 256:]
        value = jnp.concatenate([re * cs - im * sn, re * sn + im * cs], axis=0)
        main.append(value[:, :128])
        rim.append(value[:, 128:136])
    stack = jnp.concatenate(main + rim + [jnp.zeros((64, 112), F32)], axis=1)
    out = mm3(d2, halves(stack))
    even = lax.broadcasted_iota(jnp.int32, (64, 384), 0) % 2 == 0
    return jnp.concatenate(
        [(out + jnp.where(even, columns[2 * y : 2 * y + 1], columns[2 * y + 1 : 2 * y + 2])).astype(BF) for y in range(4)],
        axis=0,
    )


def regroup(lines):
    a = lax.broadcasted_iota(jnp.int32, (64, 64), 0)
    b = lax.broadcasted_iota(jnp.int32, (64, 64), 1)
    eye = jnp.where(a == b, 1.0, 0.0).astype(BF)
    turned = mm(lines, eye, 0, 0)
    main = jnp.concatenate(
        [
            jnp.concatenate([turned[32 * j : 32 * j + 32] for j in range(4)], axis=1),
            jnp.concatenate([turned[128 + 32 * j : 160 + 32 * j] for j in range(4)], axis=1),
        ],
        axis=0,
    )
    rim = jnp.concatenate(
        [jnp.concatenate([turned[256 + 8 * c + 2 * j : 258 + 8 * c + 2 * j] for j in range(4)], axis=1) for c in range(2)],
        axis=0,
    )
    return jnp.concatenate([main, rim, jnp.zeros((4, 256), F32)], axis=0).astype(BF)


def y_inverse(got, turn, zero, tk):
    lane = lax.broadcasted_iota(jnp.int32, (1, 384), 1)
    odd = (lane % 2).astype(F32)
    acc = [None] * 4
    for e in range(4):
        lines = regroup(got[e])
        part = mm(lines, tk)
        re, im = part[:, :384], part[:, 384:]
        if e == 0:
            own = lines.astype(F32)
            once = zero * (own[:, 1:2] * (1.0 - 2.0 * odd) - own[:, 0:1])
        for d in range(4):
            i = 4 * e + d
            piece = re * turn[0, i : i + 1] - im * turn[1, i : i + 1]
            acc[d] = piece + once if e == 0 else acc[d] + piece
    return jnp.concatenate(acc, axis=0)


def activations(pieces, above, center, below, point, lift18):
    mix = lax.dot_general(point, lift18, (((1,), (0,)), ((), ())), precision=lax.Precision.HIGHEST, preferred_element_type=F32)
    mix_hi, mix_lo = halves(mix)
    mix3 = jnp.concatenate([mix_hi, mix_lo, mix_hi], axis=1)
    a = lax.broadcasted_iota(jnp.int32, (64, 64), 0)
    b = lax.broadcasted_iota(jnp.int32, (64, 64), 1)
    eye = jnp.where(a == b, 1.0, 0.0).astype(BF)
    lines = jnp.concatenate([p.astype(F32)[:, 272:336] for p in pieces] + [jnp.zeros((4, 64), F32)], axis=0)
    turned = mm(eye, lines.astype(BF), 1, 1)
    moved = []
    for s in range(2):
        rows = turned[32 * s : 32 * s + 32]

        def side(k):
            return jnp.concatenate(
                [rows[30:, 2 * k : 2 * k + 2], rows[:, 2 * k + 2 : 2 * k + 4], rows[:2, 2 * k + 4 : 2 * k + 6]], axis=0
            )

        mid = jnp.concatenate([above[s], center[32 * s : 32 * s + 32], below[s]], axis=0)
        full = jnp.concatenate([mid, side(3), jnp.zeros((36, 124), F32), side(0)], axis=1)
        moved.append(jnp.concatenate([full[:, 383:], full[:, :383]], axis=1))
        moved.append(full)
        moved.append(jnp.concatenate([full[:, 1:], full[:, :1]], axis=1))
    blocks = [
        jnp.concatenate([m[r : r + 1] for m in moved] + [jnp.zeros((2, 384), F32)], axis=0) for r in range(36)
    ]
    result = []
    for i in range(34):
        view, view_lo = halves(jnp.concatenate(blocks[i : i + 3], axis=0))
        result.append(jnp.tanh(mm(mix3, jnp.concatenate([view, view, view_lo], axis=0))).astype(BF))
    mix2 = mix3[:, :48]
    return jnp.concatenate(blocks, axis=0), jnp.concatenate(result, axis=0), jnp.concatenate([mix2, mix2], axis=0)


def network(proj, planes, squash, mix4, center, out_cols):
    taps = [None] * 34
    sums = jnp.zeros((56, 128), F32)
    rest = jnp.zeros((56, 64), F32)
    for i in range(-1, 33):
        t_b = squash[(i + 1) * 64 : (i + 2) * 64]
        t = t_b.astype(F32)
        ids = (64, 66) if i < 0 else (65, 67) if i >= 32 else (i, 32 + i)
        g0 = proj[ids[0] : ids[0] + 1]
        g1 = proj[ids[1] : ids[1] + 1]
        grad = out_cols[:, 0:1] * g0 + out_cols[:, 1:2] * g1
        gz, gz_lo = halves(grad * (1.0 - t * t))
        tap = mm(mix4, jnp.concatenate([gz, gz_lo], axis=0), 0, 0)
        tap = tap[:24] + tap[24:]
        for a in range(3):
            k = i + a - 1
            if 0 <= k < 32:
                piece = tap[a * 8 : a * 8 + 8]
                taps[k] = piece if taps[k] is None else taps[k] + piece
        if 0 <= i < 32:
            view, view_lo = halves(planes[(i + 1) * 8 : (i + 4) * 8, :256])
            g_hi, g_lo = halves(jnp.concatenate([g0[:, :256], g1[:, :256]], axis=0))
            g8 = jnp.concatenate([g_hi.astype(F32), g_lo.astype(F32), jnp.zeros((4, 256), F32)], axis=0).astype(BF)
            left = jnp.concatenate([view, view_lo, g8], axis=0)
            sums = sums + mm(left, jnp.concatenate([gz[:, :256], t_b[:, :256]], axis=0), 1, 1)
            rest = rest + mm(left, gz_lo[:, :256], 1, 1)
    tail = sums[48:50, 64:] + sums[50:52, 64:]
    tail = jnp.concatenate([tail, jnp.zeros((6, 64), F32)], axis=0)
    sums = sums[:24, :64] + sums[24:48, :64] + (rest[:24] + rest[24:48])
    row = lax.broadcasted_iota(jnp.int32, (8, 64), 0)
    lane = lax.broadcasted_iota(jnp.int32, (8, 64), 1)
    for s in range(2):
        for v in range(2):
            prod = proj[32 * s : 32 * s + 32, :256] * center[32 * v : 32 * v + 32]
            total = jnp.sum(jnp.sum(prod, axis=0, keepdims=True), axis=1, keepdims=True)
            tail = jnp.where((row == 2) & (lane == 2 * s + v), total, tail)
    packed = jnp.concatenate(
        [
            jnp.concatenate([sums[0:8], sums[8:16]], axis=1),
            jnp.concatenate([sums[16:24], tail], axis=1),
        ],
        axis=0,
    )
    return jnp.concatenate(taps[:32], axis=0), jnp.concatenate([packed] * 16, axis=0)


def call(body, out_shapes, *args):
    single = not isinstance(out_shapes, (tuple, list))

    def kernel(*refs):
        ins = [ref[...] for ref in refs[: len(args)]]
        outs = body(*ins)
        for ref, value in zip(refs[len(args) :], [outs] if single else outs):
            ref[...] = value

    return pl.pallas_call(
        kernel,
        out_shape=out_shapes,
        compiler_params=pltpu.CompilerParams(vmem_limit_bytes=12 * 1024 * 1024),
    )(*args)


def call_picked(body, out_shapes, index, picked, *args):
    def kernel(index_ref, picked_ref, *refs):
        pieces = [picked_ref[index_ref[k]] for k in range(index.shape[0])]
        outs = body(pieces, *[ref[...] for ref in refs[: len(args)]])
        for ref, value in zip(refs[len(args) :], outs):
            ref[...] = value

    vmem = pl.BlockSpec(memory_space=pltpu.VMEM)
    return pl.pallas_call(
        kernel,
        in_specs=[pl.BlockSpec(memory_space=pltpu.SMEM)] + [vmem] * (1 + len(args)),
        out_specs=[vmem] * len(out_shapes),
        out_shape=out_shapes,
        compiler_params=pltpu.CompilerParams(vmem_limit_bytes=12 * 1024 * 1024),
    )(index, picked, *args)


def sds(shape, dtype):
    return jax.ShapeDtypeStruct(shape, dtype)


def exchange(value, axes):
    return lax.all_to_all(value, axes, split_axis=0, concat_axis=0)


def from_row_neighbour(value, step):
    return lax.ppermute(value, IN_W, [(i, (i + step) % WA) for i in range(WA)])


def pack_first(vel, cotangent):
    edges = jnp.concatenate([vel[:, 0:2], vel[:, 254:256], jnp.zeros((64, 124), F32)], axis=1).T[:8]
    rows = jnp.concatenate([edges, jnp.zeros((8, 192), F32)], axis=1)
    return jnp.concatenate([cotangent, rows] * 4, axis=0)


def sum_and_spread(got):
    total = got[0]
    for i in range(1, 16):
        total = total + got[i]
    return jnp.concatenate([total] * 32, axis=0)


def turns(own, cols):
    ang = TWO_PI / NY * (own * cols % NY).astype(F32)
    return jnp.stack([jnp.cos(ang), jnp.sin(ang)])


def columns_to_send(got, x, yl):
    def edges(src, first):
        rows = lax.dynamic_index_in_dim(got, src, 0, False)
        return rows[64 + first : 66 + first, :64]

    up = edges(jnp.where(yl == 3, (x + 3) % 4, x), 2)
    down = edges(jnp.where(yl == 0, (x + 1) % 4, x), 0)
    to_y = jnp.arange(4)[:, None, None]
    cols = jnp.where(to_y == (yl + 1) % 4, up, down)
    return jnp.pad(cols.reshape(8, 64), ((0, 0), (272, 48)))


def lift_matrix(lift, kernels):
    parts = []
    for a in range(3):
        for s in range(2):
            for b in range(3):
                parts.append(kernels[:, 3 * a + b] * lift[:, s])
        parts += [jnp.zeros_like(parts[0])] * 2
    return jnp.stack(parts, axis=1)


def finish_velocity(proj, taps, lift, out_w):
    hi = lax.Precision.HIGHEST
    main = proj[:64, :256].reshape(2, 32, 256)
    m2 = jnp.dot(lift.T, out_w.astype(F32).T, precision=hi)
    taps = taps.reshape(32, 8, 384)
    out = []
    for s in range(2):
        left, mid, right = taps[:, 3 * s], taps[:, 3 * s + 1], taps[:, 3 * s + 2]
        value = main[s] + m2[s, 0] * main[0] + m2[s, 1] * main[1] + mid[:, :256]
        value = value + jnp.concatenate([right[:, 383:], right[:, :255]], axis=1)
        value = value + left[:, 1:257]
        out.append(value)
    return jnp.stack(out)


def finish_weights(got, lift_rows, kernel_rows, point, out_rows, lift18_rows):
    hi = lax.Precision.HIGHEST
    total = got[0]
    for i in range(1, 32):
        total = total + got[i]
    total = total * (1.0 / math.sqrt(NX * NY))
    q = jnp.concatenate([total[:8, :64], total[:8, 64:], total[8:, :64]], axis=0)

    def pair_sum(s, v):
        return total[10:11, 64 + 2 * s + v : 65 + 2 * s + v]

    grad_out = [
        total[8 + s : 9 + s, 64:] + pair_sum(s, 0) * lift_rows[0:1] + pair_sum(s, 1) * lift_rows[1:2] for s in range(2)
    ]
    grad_point = lax.dot_general(q, lift18_rows, (((0,), (0,)), ((), ())), precision=hi, preferred_element_type=F32)
    gv = lax.dot_general(q, point, (((1,), (0,)), ((), ())), precision=hi, preferred_element_type=F32)
    grad_kernels = [
        lift_rows[0:1] * gv[8 * a : 8 * a + 3] + lift_rows[1:2] * gv[8 * a + 3 : 8 * a + 6] for a in range(3)
    ]
    grad_lift = []
    for s in range(2):
        value = out_rows[0:1] * pair_sum(0, s) + out_rows[1:2] * pair_sum(1, s)
        for a in range(3):
            first = 8 * a + 3 * s
            value = value + jnp.sum(kernel_rows[3 * a : 3 * a + 3] * gv[first : first + 3], axis=0, keepdims=True)
        grad_lift.append(value)
    return (
        jnp.concatenate(grad_lift, axis=0),
        jnp.concatenate(grad_kernels, axis=0).reshape(9, 1, 64),
        grad_point,
        jnp.concatenate(grad_out, axis=0),
    )


def local(velocity, cotangent, lift_weight, depth_kernels, point_weights, out_weight):
    tab = make_tables()
    x, yl, yh, z, core = (lax.axis_index(a) for a in AXES)
    w = 16 * yh + 2 * z + core
    kernels = depth_kernels[0]
    point = point_weights[0]
    col = jnp.arange(256)[None, :]
    step = jnp.arange(16)[:, None]
    klass = x + 4 * (step // 4)
    turn1 = turns(klass, col + 1024 * (step % 4) + 256 * yl)
    sign = jnp.where(x == 0, (1 - 2 * (col % 2)).astype(F32), 0.0)
    zero = jnp.where(x == 0, jnp.ones((1, 384), F32), 0.0)
    ky_lane = (x + 4 * yl + 16 * (4 * w + jnp.arange(128) // 32)).astype(F32)[None, :]
    cols4 = jnp.asarray(COL_ID.astype(np.int32))[None, :]
    turn4 = turns(klass, cols4 + 1024 * (step % 4) + 256 * yl + NY)
    lift18 = lift_matrix(lift_weight, kernels)

    sent1 = call(pack_first, sds((288, 256), F32), velocity.reshape(64, 256), cotangent.reshape(64, 256))
    got1 = exchange(sent1.reshape(4, 72, 256), ("x",))
    spec = call(y_forward, sds((128, 2, 256), F32), got1, turn1, sign, tab["t1"])
    spec, bottom = lax.optimization_barrier((spec, velocity[:, 30:]))
    got2 = exchange(spec, ("yl",) + IN_W)
    above = from_row_neighbour(bottom, 1)
    columns = columns_to_send(got1, x, yl)
    sent3 = call(
        x_project, sds((256, 384), BF), got2.reshape(4, 64, 256), ky_lane, columns, tab["d1"], tab["tw1"], tab["kr"], tab["ik"], tab["tw2"], tab["d2"]
    )
    sent3, above, top = lax.optimization_barrier((sent3, above, velocity[:, :2]))
    below = from_row_neighbour(top, -1)
    got3 = exchange(sent3.reshape(128, 2, 384), ("yl",) + IN_W)
    sent4 = call(y_inverse, sds((288, 384), F32), got3.reshape(4, 64, 384), turn4, zero, tab["tk"])
    sent4, below = lax.optimization_barrier((sent4, below))
    got4 = exchange(sent4.reshape(4, 72, 384), ("x",))
    point_f = point.astype(F32)
    out_cols = out_weight.astype(F32).T
    center = velocity.reshape(64, 256)
    near = [((yl + dy) % 4) * WA + (w + dw) % WA for dy in (3, 1) for dw in (31, 0, 1)]
    planes, squash, mix4 = call_picked(
        activations,
        (sds((288, 384), F32), sds((34 * 64, 384), BF), sds((128, 48), BF)),
        jnp.stack(near).astype(jnp.int32), got3, above, center, below, point_f, lift18,
    )

    def last(got, *rest):
        proj = (got[0] + got[1]) + (got[2] + got[3])
        return (proj,) + network(proj, *rest)

    proj, taps, packed = call(
        last,
        (sds((72, 384), F32), sds((256, 384), F32), sds((256, 128), F32)),
        got4, planes, squash, mix4, center, out_cols,
    )
    part = exchange(packed.reshape(16, 16, 128), ("yl", "yh", "c"))
    part = call(sum_and_spread, sds((512, 128), F32), part)
    total = exchange(part.reshape(32, 16, 128), ("x", "z"))
    grad_velocity = finish_velocity(proj, taps, lift_weight, out_weight)
    grad_lift, grad_kernels, grad_point, grad_out = call(
        finish_weights,
        (sds((2, 64), F32), sds((9, 1, 64), F32), sds((64, 64), F32), sds((2, 64), F32)),
        total, lift_weight.T, kernels.T, point_f, out_weight.astype(F32), lift18.T,
    )
    return grad_velocity, grad_lift.T, grad_kernels.transpose(1, 2, 0), grad_point[None], grad_out


def solution(mesh):
    split = jax.sharding.Mesh(mesh.devices.reshape(SIZES), AXES)
    field = P(None, IN_W, IN_H)
    return jax.shard_map(
        local,
        mesh=split,
        in_specs=(field, field, P(), P(), P(), P()),
        out_specs=(field, P(), P(), P(), P()),
        check_vma=False,
    )
```

```python
import math

import jax
import jax.numpy as jnp
import ml_dtypes
import numpy as np
from jax import lax
from jax.experimental import pallas as pl
from jax.experimental.pallas import tpu as pltpu
from jax.sharding import PartitionSpec as P

BF = jnp.bfloat16
F32 = jnp.float32
HA, WA = 16, 32
AXES = ("x", "yl", "yh", "z", "c")
SIZES = (4, 4, 2, 8, 2)
IN_H = ("x", "yl")
IN_W = ("yh", "z", "c")
ROWS, COLS = 32, 256
NX, NY = WA * ROWS, HA * COLS
TWO_PI = 2.0 * math.pi
COL_ID = np.concatenate([np.arange(257), np.zeros(126, np.int64), [-1]])
COL_USED = np.concatenate([np.ones(257), np.zeros(126), [1]])


def bf(table):
    return np.asarray(table).astype(ml_dtypes.bfloat16)


def pair(table):
    high = bf(table)
    return np.stack([high, bf(table - high.astype(np.float64))])


def make_tables():
    r = np.arange(256)
    k2 = np.arange(128)
    ang = TWO_PI * (np.outer(k2, r) % 256) / 256
    c, s = np.cos(ang), np.sin(ang)
    t1 = np.stack([np.concatenate([c, s], 1), np.concatenate([-s, c], 1)], 1)
    t1 = t1.reshape(32, 4, 2, 512).transpose(1, 0, 2, 3).reshape(256, 512)

    n32 = np.arange(32)
    a32 = TWO_PI * (np.outer(n32, n32) % 32) / 32
    c32, s32 = np.cos(a32), np.sin(a32)
    d1 = np.zeros((4, 32, 32, 2))
    d1[0, :, :, 0] = c32
    d1[1, :, :, 0] = -s32
    d1[2, :, :, 1] = c32
    d1[3, :, :, 1] = -s32
    d1 = d1.reshape(128, 64)
    tw = TWO_PI * np.outer(n32, np.tile(n32, 8)) / 1024
    tw1 = np.stack([np.cos(tw), np.sin(tw)]).astype(np.float32)

    kr = np.zeros((2, 4, 32, 2, 4, 32))
    ik = np.zeros((2, 4, 32, 2, 256))
    rows = np.concatenate([n32, [-1, 32]])
    a = TWO_PI * np.outer(n32, rows) / 32
    row_of = np.zeros(256)
    for j in range(4):
        kr[0, j, :, 0, j, :] = c32
        kr[1, j, :, 0, j, :] = s32
        kr[1, j, :, 1, j, :] = c32
        kr[0, j, :, 1, j, :] = -s32
        lanes = list(range(j * 32, j * 32 + 32)) + [128 + j * 2, 129 + j * 2]
        row_of[lanes] = rows
        ik[0, j, :, 0, lanes] = np.cos(a).T
        ik[1, j, :, 0, lanes] = -np.sin(a).T
        ik[0, j, :, 1, lanes] = np.sin(a).T
        ik[1, j, :, 1, lanes] = np.cos(a).T
    kr = kr.reshape(256, 256)
    ik = ik.reshape(256, 512)
    tw = TWO_PI * np.outer(n32, row_of) / 1024
    tw2 = np.stack([np.cos(tw), np.sin(tw)]).astype(np.float32)
    d2 = np.zeros((32, 2, 2, 32))
    d2[:, 0, 0] = c32
    d2[:, 0, 1] = -s32
    d2[:, 1, 0] = s32
    d2[:, 1, 1] = c32
    d2 = d2.reshape(64, 64)

    ang = TWO_PI * (np.outer(k2, COL_ID) % 256) / 256
    tk = np.zeros((128, 2, 2, 384))
    tk[:, 0, 0] = 2 * np.cos(ang) * COL_USED
    tk[:, 1, 0] = -2 * np.sin(ang) * COL_USED
    tk[:, 0, 1] = 2 * np.sin(ang) * COL_USED
    tk[:, 1, 1] = 2 * np.cos(ang) * COL_USED
    tk = tk.reshape(32, 4, 2, 768).transpose(1, 0, 2, 3).reshape(256, 768)
    return dict(t1=pair(t1), d1=pair(d1), tw1=tw1, kr=pair(kr), ik=pair(ik), tw2=tw2, d2=pair(d2), tk=bf(tk))


def mm(a, b, ca=1, cb=0):
    return lax.dot_general(a, b, (((ca,), (cb,)), ((), ())), preferred_element_type=F32)


def halves(value):
    high = value.astype(BF)
    return high, (value - high.astype(F32)).astype(BF)


def mm3(a, b, ca=1, cb=0):
    return mm(a[0], b[0], ca, cb) + (mm(a[1], b[0], ca, cb) + mm(a[0], b[1], ca, cb))


def y_forward(got, turn, sign, t1):
    parts = [got[q, :64] for q in range(4)]
    row = lax.broadcasted_iota(jnp.int32, (64, 256), 0)
    pick = jnp.where(row == 1, sign, 0.0).astype(BF)
    result = []
    for e in range(4):
        re = sum(parts[q] * turn[0, 4 * e + q : 4 * e + q + 1] for q in range(4))
        im = -sum(parts[q] * turn[1, 4 * e + q : 4 * e + q + 1] for q in range(4))
        both = halves(jnp.concatenate([re, im], axis=1))
        out = []
        for j in range(4):
            block = mm3((t1[0, j * 64 : (j + 1) * 64], t1[1, j * 64 : (j + 1) * 64]), both, 1, 1)
            if e == 0 and j == 0:
                block = block + mm(pick, both[0][:, :256], 1, 1) + mm(pick, both[1][:, :256], 1, 1)
            out.append(block)
        pieces = [out[j][:, 32 * c : 32 * c + 32] for c in range(2) for j in range(4)]
        result.append(jnp.concatenate(pieces, axis=1))
    return jnp.concatenate(result, axis=0).reshape(128, 2, 256)


def x_project(lines, ky_lane, columns, d1, tw1, kr, ik, tw2, d2):
    first = mm3(d1, halves((lines[0] + lines[1]) + (lines[2] + lines[3])))
    cs, sn = tw1[0], tw1[1]
    turned = []
    for c in range(2):
        for p in range(2):
            re = first[64 * p : 64 * p + 32]
            im = first[64 * p + 32 : 64 * p + 64]
            span = slice(128 * c, 128 * c + 128)
            turned.append(
                jnp.concatenate([(re * cs + im * sn)[:, span], (im * cs - re * sn)[:, span]], axis=1)
            )
    spec = mm3(halves(jnp.concatenate(turned, axis=0)), kr)
    lane = lax.broadcasted_iota(jnp.int32, (32, 128), 1)
    kx = lax.broadcasted_iota(jnp.int32, (32, 128), 0) + 32 * (lane % 32)
    kx = jnp.where(2 * kx >= NX, kx - NX, kx).astype(F32)
    ky = jnp.broadcast_to(ky_lane, (32, 128))
    edge_x = kx == -float(NX // 2)

    def factors(wave_y, edge_y):
        inv = 1.0 / jnp.maximum(kx * kx + wave_y * wave_y, 1.0)
        scale = 1.0 / float(NX * NY)
        cross = jnp.where(edge_x != edge_y, 0.0, -kx * wave_y * inv)
        return (1.0 - kx * kx * inv) * scale, cross * scale, (1.0 - wave_y * wave_y * inv) * scale

    ar, br, dr = factors(ky, jnp.zeros((32, 128), jnp.bool_))
    packed = ky == 0.0
    ai, bi, di = factors(jnp.where(packed, -float(NY // 2), ky), packed)
    (r0, r0i), (i0, i0i), (r1, r1i), (i1, i1i) = (
        (spec[32 * i : 32 * i + 32, :128], spec[32 * i : 32 * i + 32, 128:]) for i in range(4)
    )
    first = jnp.concatenate(
        [ar * r0 + br * r1 - (ai * i0i + bi * i1i), ar * r0i + br * r1i + ai * i0 + bi * i1], axis=1
    )
    second = jnp.concatenate(
        [br * r0 + dr * r1 - (bi * i0i + di * i1i), br * r0i + dr * r1i + bi * i0 + di * i1], axis=1
    )
    back = mm3(halves(jnp.concatenate([first, second], axis=0)), ik)
    cs, sn = tw2[0], tw2[1]
    main, rim = [], []
    for c in range(2):
        re = back[32 * c : 32 * c + 32, :256]
        im = back[32 * c : 32 * c + 32, 256:]
        value = jnp.concatenate([re * cs - im * sn, re * sn + im * cs], axis=0)
        main.append(value[:, :128])
        rim.append(value[:, 128:136])
    stack = jnp.concatenate(main + rim + [jnp.zeros((64, 112), F32)], axis=1)
    out = mm3(d2, halves(stack))
    even = lax.broadcasted_iota(jnp.int32, (64, 384), 0) % 2 == 0
    return jnp.concatenate(
        [(out + jnp.where(even, columns[2 * y : 2 * y + 1], columns[2 * y + 1 : 2 * y + 2])).astype(BF) for y in range(4)],
        axis=0,
    )


def regroup(lines):
    a = lax.broadcasted_iota(jnp.int32, (64, 64), 0)
    b = lax.broadcasted_iota(jnp.int32, (64, 64), 1)
    eye = jnp.where(a == b, 1.0, 0.0).astype(BF)
    turned = mm(lines, eye, 0, 0)
    main = jnp.concatenate(
        [
            jnp.concatenate([turned[32 * j : 32 * j + 32] for j in range(4)], axis=1),
            jnp.concatenate([turned[128 + 32 * j : 160 + 32 * j] for j in range(4)], axis=1),
        ],
        axis=0,
    )
    rim = jnp.concatenate(
        [jnp.concatenate([turned[256 + 8 * c + 2 * j : 258 + 8 * c + 2 * j] for j in range(4)], axis=1) for c in range(2)],
        axis=0,
    )
    return jnp.concatenate([main, rim, jnp.zeros((4, 256), F32)], axis=0).astype(BF)


def y_inverse(got, turn, zero, tk):
    lane = lax.broadcasted_iota(jnp.int32, (1, 384), 1)
    odd = (lane % 2).astype(F32)
    acc = [None] * 4
    for e in range(4):
        lines = regroup(got[e])
        part = mm(lines, tk)
        re, im = part[:, :384], part[:, 384:]
        if e == 0:
            own = lines.astype(F32)
            once = zero * (own[:, 1:2] * (1.0 - 2.0 * odd) - own[:, 0:1])
        for d in range(4):
            i = 4 * e + d
            piece = re * turn[0, i : i + 1] - im * turn[1, i : i + 1]
            acc[d] = piece + once if e == 0 else acc[d] + piece
    return jnp.concatenate(acc, axis=0)


def activations(pieces, above, center, below, point, lift18):
    mix = lax.dot_general(point, lift18, (((1,), (0,)), ((), ())), precision=lax.Precision.HIGHEST, preferred_element_type=F32)
    mix_hi, mix_lo = halves(mix)
    mix3 = jnp.concatenate([mix_hi, mix_lo, mix_hi], axis=1)
    a = lax.broadcasted_iota(jnp.int32, (64, 64), 0)
    b = lax.broadcasted_iota(jnp.int32, (64, 64), 1)
    eye = jnp.where(a == b, 1.0, 0.0).astype(BF)
    lines = jnp.concatenate([p.astype(F32)[:, 272:336] for p in pieces] + [jnp.zeros((4, 64), F32)], axis=0)
    turned = mm(eye, lines.astype(BF), 1, 1)
    moved = []
    for s in range(2):
        rows = turned[32 * s : 32 * s + 32]

        def side(k):
            return jnp.concatenate(
                [rows[30:, 2 * k : 2 * k + 2], rows[:, 2 * k + 2 : 2 * k + 4], rows[:2, 2 * k + 4 : 2 * k + 6]], axis=0
            )

        mid = jnp.concatenate([above[s], center[32 * s : 32 * s + 32], below[s]], axis=0)
        full = jnp.concatenate([mid, side(3), jnp.zeros((36, 124), F32), side(0)], axis=1)
        moved.append(jnp.concatenate([full[:, 383:], full[:, :383]], axis=1))
        moved.append(full)
        moved.append(jnp.concatenate([full[:, 1:], full[:, :1]], axis=1))
    blocks = [
        jnp.concatenate([m[r : r + 1] for m in moved] + [jnp.zeros((2, 384), F32)], axis=0) for r in range(36)
    ]
    result = []
    for i in range(34):
        view, view_lo = halves(jnp.concatenate(blocks[i : i + 3], axis=0))
        result.append(jnp.tanh(mm(mix3, jnp.concatenate([view, view, view_lo], axis=0))).astype(BF))
    mix2 = mix3[:, :48]
    return jnp.concatenate(blocks, axis=0), jnp.concatenate(result, axis=0), jnp.concatenate([mix2, mix2], axis=0)


def network(proj, planes, squash, mix4, center, out_cols):
    taps = [None] * 34
    sums = jnp.zeros((56, 128), F32)
    rest = jnp.zeros((56, 64), F32)
    for i in range(-1, 33):
        t_b = squash[(i + 1) * 64 : (i + 2) * 64]
        t = t_b.astype(F32)
        ids = (64, 66) if i < 0 else (65, 67) if i >= 32 else (i, 32 + i)
        g0 = proj[ids[0] : ids[0] + 1]
        g1 = proj[ids[1] : ids[1] + 1]
        grad = out_cols[:, 0:1] * g0 + out_cols[:, 1:2] * g1
        gz, gz_lo = halves(grad * (1.0 - t * t))
        tap = mm(mix4, jnp.concatenate([gz, gz_lo], axis=0), 0, 0)
        tap = tap[:24] + tap[24:]
        for a in range(3):
            k = i + a - 1
            if 0 <= k < 32:
                piece = tap[a * 8 : a * 8 + 8]
                taps[k] = piece if taps[k] is None else taps[k] + piece
        if 0 <= i < 32:
            view, view_lo = halves(planes[(i + 1) * 8 : (i + 4) * 8, :256])
            g_hi, g_lo = halves(jnp.concatenate([g0[:, :256], g1[:, :256]], axis=0))
            g8 = jnp.concatenate([g_hi.astype(F32), g_lo.astype(F32), jnp.zeros((4, 256), F32)], axis=0).astype(BF)
            left = jnp.concatenate([view, view_lo, g8], axis=0)
            sums = sums + mm(left, jnp.concatenate([gz[:, :256], t_b[:, :256]], axis=0), 1, 1)
            rest = rest + mm(left, gz_lo[:, :256], 1, 1)
    tail = sums[48:50, 64:] + sums[50:52, 64:]
    tail = jnp.concatenate([tail, jnp.zeros((6, 64), F32)], axis=0)
    sums = sums[:24, :64] + sums[24:48, :64] + (rest[:24] + rest[24:48])
    row = lax.broadcasted_iota(jnp.int32, (8, 64), 0)
    lane = lax.broadcasted_iota(jnp.int32, (8, 64), 1)
    for s in range(2):
        for v in range(2):
            prod = proj[32 * s : 32 * s + 32, :256] * center[32 * v : 32 * v + 32]
            total = jnp.sum(jnp.sum(prod, axis=0, keepdims=True), axis=1, keepdims=True)
            tail = jnp.where((row == 2) & (lane == 2 * s + v), total, tail)
    packed = jnp.concatenate(
        [
            jnp.concatenate([sums[0:8], sums[8:16]], axis=1),
            jnp.concatenate([sums[16:24], tail], axis=1),
        ],
        axis=0,
    )
    return jnp.concatenate(taps[:32], axis=0), jnp.concatenate([packed] * 16, axis=0)


def call(body, out_shapes, *args):
    single = not isinstance(out_shapes, (tuple, list))

    def kernel(*refs):
        ins = [ref[...] for ref in refs[: len(args)]]
        outs = body(*ins)
        for ref, value in zip(refs[len(args) :], [outs] if single else outs):
            ref[...] = value

    return pl.pallas_call(
        kernel,
        out_shape=out_shapes,
        compiler_params=pltpu.CompilerParams(vmem_limit_bytes=12 * 1024 * 1024),
    )(*args)


def call_picked(body, out_shapes, index, picked, *args):
    def kernel(index_ref, picked_ref, *refs):
        pieces = [picked_ref[index_ref[k]] for k in range(index.shape[0])]
        outs = body(pieces, *[ref[...] for ref in refs[: len(args)]])
        for ref, value in zip(refs[len(args) :], outs):
            ref[...] = value

    vmem = pl.BlockSpec(memory_space=pltpu.VMEM)
    return pl.pallas_call(
        kernel,
        in_specs=[pl.BlockSpec(memory_space=pltpu.SMEM)] + [vmem] * (1 + len(args)),
        out_specs=[vmem] * len(out_shapes),
        out_shape=out_shapes,
        compiler_params=pltpu.CompilerParams(vmem_limit_bytes=12 * 1024 * 1024),
    )(index, picked, *args)


def sds(shape, dtype):
    return jax.ShapeDtypeStruct(shape, dtype)


def exchange(value, axes):
    return lax.all_to_all(value, axes, split_axis=0, concat_axis=0)


def from_row_neighbour(value, step):
    return lax.ppermute(value, IN_W, [(i, (i + step) % WA) for i in range(WA)])


def pack_first(vel, cotangent):
    def kernel(vel_ref, cot_ref, out_ref, rows_ref, edge_ref, sems):
        load = pltpu.make_async_copy(vel_ref, rows_ref, sems.at[0])
        load.start()
        moves = [pltpu.make_async_copy(cot_ref, out_ref.at[d, pl.ds(0, 64)], sems.at[1 + d]) for d in range(4)]
        for move in moves:
            move.start()
        load.wait()
        rows = rows_ref[...]
        edges = jnp.concatenate([rows[:, 0:2], rows[:, 254:256], jnp.zeros((64, 124), F32)], axis=1).T[:8]
        edge_ref[...] = jnp.concatenate([edges, jnp.zeros((8, 192), F32)], axis=1)
        ends = [pltpu.make_async_copy(edge_ref, out_ref.at[d, pl.ds(64, 8)], sems.at[5 + d]) for d in range(4)]
        for move in ends:
            move.start()
        for move in moves + ends:
            move.wait()

    anywhere = pl.BlockSpec(memory_space=pl.ANY)
    return pl.pallas_call(
        kernel,
        in_specs=[anywhere, anywhere],
        out_specs=anywhere,
        out_shape=sds((4, 72, 256), F32),
        scratch_shapes=[pltpu.VMEM((64, 256), F32), pltpu.VMEM((8, 256), F32), pltpu.SemaphoreType.DMA((9,))],
    )(vel, cotangent)


def sum_and_spread(got):
    total = got[0]
    for i in range(1, 16):
        total = total + got[i]
    return jnp.concatenate([total] * 32, axis=0)


def turns(own, cols):
    ang = TWO_PI / NY * (own * cols % NY).astype(F32)
    return jnp.stack([jnp.cos(ang), jnp.sin(ang)])


def columns_to_send(got, x, yl):
    def edges(src, first):
        rows = lax.dynamic_index_in_dim(got, src, 0, False)
        return rows[64 + first : 66 + first, :64]

    up = edges(jnp.where(yl == 3, (x + 3) % 4, x), 2)
    down = edges(jnp.where(yl == 0, (x + 1) % 4, x), 0)
    to_y = jnp.arange(4)[:, None, None]
    cols = jnp.where(to_y == (yl + 1) % 4, up, down)
    return jnp.pad(cols.reshape(8, 64), ((0, 0), (272, 48)))


def lift_matrix(lift, kernels):
    parts = []
    for a in range(3):
        for s in range(2):
            for b in range(3):
                parts.append(kernels[:, 3 * a + b] * lift[:, s])
        parts += [jnp.zeros_like(parts[0])] * 2
    return jnp.stack(parts, axis=1)


def finish_velocity(proj, taps, lift, out_w):
    hi = lax.Precision.HIGHEST
    main = proj[:64, :256].reshape(2, 32, 256)
    m2 = jnp.dot(lift.T, out_w.astype(F32).T, precision=hi)
    taps = taps.reshape(32, 8, 384)
    out = []
    for s in range(2):
        left, mid, right = taps[:, 3 * s], taps[:, 3 * s + 1], taps[:, 3 * s + 2]
        value = main[s] + m2[s, 0] * main[0] + m2[s, 1] * main[1] + mid[:, :256]
        value = value + jnp.concatenate([right[:, 383:], right[:, :255]], axis=1)
        value = value + left[:, 1:257]
        out.append(value)
    return jnp.stack(out)


def finish_weights(got, lift_rows, kernel_rows, point, out_rows, lift18_rows):
    hi = lax.Precision.HIGHEST
    total = got[0]
    for i in range(1, 32):
        total = total + got[i]
    total = total * (1.0 / math.sqrt(NX * NY))
    q = jnp.concatenate([total[:8, :64], total[:8, 64:], total[8:, :64]], axis=0)

    def pair_sum(s, v):
        return total[10:11, 64 + 2 * s + v : 65 + 2 * s + v]

    grad_out = [
        total[8 + s : 9 + s, 64:] + pair_sum(s, 0) * lift_rows[0:1] + pair_sum(s, 1) * lift_rows[1:2] for s in range(2)
    ]
    grad_point = lax.dot_general(q, lift18_rows, (((0,), (0,)), ((), ())), precision=hi, preferred_element_type=F32)
    gv = lax.dot_general(q, point, (((1,), (0,)), ((), ())), precision=hi, preferred_element_type=F32)
    grad_kernels = [
        lift_rows[0:1] * gv[8 * a : 8 * a + 3] + lift_rows[1:2] * gv[8 * a + 3 : 8 * a + 6] for a in range(3)
    ]
    grad_lift = []
    for s in range(2):
        value = out_rows[0:1] * pair_sum(0, s) + out_rows[1:2] * pair_sum(1, s)
        for a in range(3):
            first = 8 * a + 3 * s
            value = value + jnp.sum(kernel_rows[3 * a : 3 * a + 3] * gv[first : first + 3], axis=0, keepdims=True)
        grad_lift.append(value)
    return (
        jnp.concatenate(grad_lift, axis=0),
        jnp.concatenate(grad_kernels, axis=0).reshape(9, 1, 64),
        grad_point,
        jnp.concatenate(grad_out, axis=0),
    )


def local(velocity, cotangent, lift_weight, depth_kernels, point_weights, out_weight):
    tab = make_tables()
    x, yl, yh, z, core = (lax.axis_index(a) for a in AXES)
    w = 16 * yh + 2 * z + core
    kernels = depth_kernels[0]
    point = point_weights[0]
    col = jnp.arange(256)[None, :]
    step = jnp.arange(16)[:, None]
    klass = x + 4 * (step // 4)
    turn1 = turns(klass, col + 1024 * (step % 4) + 256 * yl)
    sign = jnp.where(x == 0, (1 - 2 * (col % 2)).astype(F32), 0.0)
    zero = jnp.where(x == 0, jnp.ones((1, 384), F32), 0.0)
    ky_lane = (x + 4 * yl + 16 * (4 * w + jnp.arange(128) // 32)).astype(F32)[None, :]
    cols4 = jnp.asarray(COL_ID.astype(np.int32))[None, :]
    turn4 = turns(klass, cols4 + 1024 * (step % 4) + 256 * yl + NY)
    lift18 = lift_matrix(lift_weight, kernels)

    got1 = exchange(pack_first(velocity.reshape(64, 256), cotangent.reshape(64, 256)), ("x",))
    spec = call(y_forward, sds((128, 2, 256), F32), got1, turn1, sign, tab["t1"])
    spec, bottom = lax.optimization_barrier((spec, velocity[:, 30:]))
    got2 = exchange(spec, ("yl",) + IN_W)
    above = from_row_neighbour(bottom, 1)
    columns = columns_to_send(got1, x, yl)
    sent3 = call(
        x_project, sds((256, 384), BF), got2.reshape(4, 64, 256), ky_lane, columns, tab["d1"], tab["tw1"], tab["kr"], tab["ik"], tab["tw2"], tab["d2"]
    )
    sent3, above, top = lax.optimization_barrier((sent3, above, velocity[:, :2]))
    below = from_row_neighbour(top, -1)
    got3 = exchange(sent3.reshape(128, 2, 384), ("yl",) + IN_W)
    sent4 = call(y_inverse, sds((288, 384), F32), got3.reshape(4, 64, 384), turn4, zero, tab["tk"])
    sent4, below = lax.optimization_barrier((sent4, below))
    got4 = exchange(sent4.reshape(4, 72, 384), ("x",))
    point_f = point.astype(F32)
    out_cols = out_weight.astype(F32).T
    center = velocity.reshape(64, 256)
    near = [((yl + dy) % 4) * WA + (w + dw) % WA for dy in (3, 1) for dw in (31, 0, 1)]
    planes, squash, mix4 = call_picked(
        activations,
        (sds((288, 384), F32), sds((34 * 64, 384), BF), sds((128, 48), BF)),
        jnp.stack(near).astype(jnp.int32), got3, above, center, below, point_f, lift18,
    )

    def last(got, *rest):
        proj = (got[0] + got[1]) + (got[2] + got[3])
        return (proj,) + network(proj, *rest)

    proj, taps, packed = call(
        last,
        (sds((72, 384), F32), sds((256, 384), F32), sds((256, 128), F32)),
        got4, planes, squash, mix4, center, out_cols,
    )
    part = exchange(packed.reshape(16, 16, 128), ("yl", "yh", "c"))
    part = call(sum_and_spread, sds((512, 128), F32), part)
    total = exchange(part.reshape(32, 16, 128), ("x", "z"))
    grad_velocity = finish_velocity(proj, taps, lift_weight, out_weight)
    grad_lift, grad_kernels, grad_point, grad_out = call(
        finish_weights,
        (sds((2, 64), F32), sds((9, 1, 64), F32), sds((64, 64), F32), sds((2, 64), F32)),
        total, lift_weight.T, kernels.T, point_f, out_weight.astype(F32), lift18.T,
    )
    return grad_velocity, grad_lift.T, grad_kernels.transpose(1, 2, 0), grad_point[None], grad_out


def solution(mesh):
    split = jax.sharding.Mesh(mesh.devices.reshape(SIZES), AXES)
    field = P(None, IN_W, IN_H)
    return jax.shard_map(
        local,
        mesh=split,
        in_specs=(field, field, P(), P(), P(), P()),
        out_specs=(field, P(), P(), P(), P()),
        check_vma=False,
    )
```

```python
import math

import jax
import jax.numpy as jnp
import ml_dtypes
import numpy as np
from jax import lax
from jax.experimental import pallas as pl
from jax.experimental.pallas import tpu as pltpu
from jax.sharding import PartitionSpec as P

BF = jnp.bfloat16
F32 = jnp.float32
HA, WA = 16, 32
AXES = ("x", "yl", "yh", "z", "c")
SIZES = (4, 4, 2, 8, 2)
IN_H = ("x", "yl")
IN_W = ("yh", "z", "c")
ROWS, COLS = 32, 256
NX, NY = WA * ROWS, HA * COLS
TWO_PI = 2.0 * math.pi
COL_ID = np.concatenate([np.arange(257), np.zeros(126, np.int64), [-1]])
COL_USED = np.concatenate([np.ones(257), np.zeros(126), [1]])


def bf(table):
    return np.asarray(table).astype(ml_dtypes.bfloat16)


def pair(table):
    high = bf(table)
    return np.stack([high, bf(table - high.astype(np.float64))])


def make_tables():
    r = np.arange(256)
    k2 = np.arange(128)
    ang = TWO_PI * (np.outer(k2, r) % 256) / 256
    c, s = np.cos(ang), np.sin(ang)
    t1 = np.stack([np.concatenate([c, s], 1), np.concatenate([-s, c], 1)], 1)
    t1 = t1.reshape(32, 4, 2, 512).transpose(1, 0, 2, 3).reshape(256, 512)

    n32 = np.arange(32)
    a32 = TWO_PI * (np.outer(n32, n32) % 32) / 32
    c32, s32 = np.cos(a32), np.sin(a32)
    d1 = np.zeros((4, 32, 32, 2))
    d1[0, :, :, 0] = c32
    d1[1, :, :, 0] = -s32
    d1[2, :, :, 1] = c32
    d1[3, :, :, 1] = -s32
    d1 = d1.reshape(128, 64)
    tw = TWO_PI * np.outer(n32, np.tile(n32, 8)) / 1024
    tw1 = np.stack([np.cos(tw), np.sin(tw)]).astype(np.float32)

    kr = np.zeros((2, 4, 32, 2, 4, 32))
    ik = np.zeros((2, 4, 32, 2, 256))
    rows = np.concatenate([n32, [-1, 32]])
    a = TWO_PI * np.outer(n32, rows) / 32
    row_of = np.zeros(256)
    for j in range(4):
        kr[0, j, :, 0, j, :] = c32
        kr[1, j, :, 0, j, :] = s32
        kr[1, j, :, 1, j, :] = c32
        kr[0, j, :, 1, j, :] = -s32
        lanes = list(range(j * 32, j * 32 + 32)) + [128 + j * 2, 129 + j * 2]
        row_of[lanes] = rows
        ik[0, j, :, 0, lanes] = np.cos(a).T
        ik[1, j, :, 0, lanes] = -np.sin(a).T
        ik[0, j, :, 1, lanes] = np.sin(a).T
        ik[1, j, :, 1, lanes] = np.cos(a).T
    kr = kr.reshape(256, 256)
    ik = ik.reshape(256, 512)
    tw = TWO_PI * np.outer(n32, row_of) / 1024
    tw2 = np.stack([np.cos(tw), np.sin(tw)]).astype(np.float32)
    d2 = np.zeros((32, 2, 2, 32))
    d2[:, 0, 0] = c32
    d2[:, 0, 1] = -s32
    d2[:, 1, 0] = s32
    d2[:, 1, 1] = c32
    d2 = d2.reshape(64, 64)

    ang = TWO_PI * (np.outer(k2, COL_ID) % 256) / 256
    tk = np.zeros((128, 2, 2, 384))
    tk[:, 0, 0] = 2 * np.cos(ang) * COL_USED
    tk[:, 1, 0] = -2 * np.sin(ang) * COL_USED
    tk[:, 0, 1] = 2 * np.sin(ang) * COL_USED
    tk[:, 1, 1] = 2 * np.cos(ang) * COL_USED
    tk = tk.reshape(32, 4, 2, 768).transpose(1, 0, 2, 3).reshape(256, 768)
    return dict(t1=pair(t1), d1=pair(d1), tw1=tw1, kr=pair(kr), ik=pair(ik), tw2=tw2, d2=pair(d2), tk=bf(tk))


def mm(a, b, ca=1, cb=0):
    return lax.dot_general(a, b, (((ca,), (cb,)), ((), ())), preferred_element_type=F32)


def halves(value):
    high = value.astype(BF)
    return high, (value - high.astype(F32)).astype(BF)


def mm3(a, b, ca=1, cb=0):
    return mm(a[0], b[0], ca, cb) + (mm(a[1], b[0], ca, cb) + mm(a[0], b[1], ca, cb))


def y_forward(got, turn, sign, t1):
    parts = [got[q, :64] for q in range(4)]
    row = lax.broadcasted_iota(jnp.int32, (64, 256), 0)
    pick = jnp.where(row == 1, sign, 0.0).astype(BF)
    result = []
    for e in range(4):
        re = sum(parts[q] * turn[0, 4 * e + q : 4 * e + q + 1] for q in range(4))
        im = -sum(parts[q] * turn[1, 4 * e + q : 4 * e + q + 1] for q in range(4))
        both = halves(jnp.concatenate([re, im], axis=1))
        out = []
        for j in range(4):
            block = mm3((t1[0, j * 64 : (j + 1) * 64], t1[1, j * 64 : (j + 1) * 64]), both, 1, 1)
            if e == 0 and j == 0:
                block = block + mm(pick, both[0][:, :256], 1, 1) + mm(pick, both[1][:, :256], 1, 1)
            out.append(block)
        pieces = [out[j][:, 32 * c : 32 * c + 32] for c in range(2) for j in range(4)]
        result.append(jnp.concatenate(pieces, axis=1))
    return jnp.concatenate(result, axis=0).reshape(128, 2, 256)


def x_project(lines, ky_lane, columns, d1, tw1, kr, ik, tw2, d2):
    first = mm3(d1, halves((lines[0] + lines[1]) + (lines[2] + lines[3])))
    cs, sn = tw1[0], tw1[1]
    turned = []
    for c in range(2):
        for p in range(2):
            re = first[64 * p : 64 * p + 32]
            im = first[64 * p + 32 : 64 * p + 64]
            span = slice(128 * c, 128 * c + 128)
            turned.append(
                jnp.concatenate([(re * cs + im * sn)[:, span], (im * cs - re * sn)[:, span]], axis=1)
            )
    spec = mm3(halves(jnp.concatenate(turned, axis=0)), kr)
    lane = lax.broadcasted_iota(jnp.int32, (32, 128), 1)
    kx = lax.broadcasted_iota(jnp.int32, (32, 128), 0) + 32 * (lane % 32)
    kx = jnp.where(2 * kx >= NX, kx - NX, kx).astype(F32)
    ky = jnp.broadcast_to(ky_lane, (32, 128))
    edge_x = kx == -float(NX // 2)

    def factors(wave_y, edge_y):
        inv = 1.0 / jnp.maximum(kx * kx + wave_y * wave_y, 1.0)
        scale = 1.0 / float(NX * NY)
        cross = jnp.where(edge_x != edge_y, 0.0, -kx * wave_y * inv)
        return (1.0 - kx * kx * inv) * scale, cross * scale, (1.0 - wave_y * wave_y * inv) * scale

    ar, br, dr = factors(ky, jnp.zeros((32, 128), jnp.bool_))
    packed = ky == 0.0
    ai, bi, di = factors(jnp.where(packed, -float(NY // 2), ky), packed)
    (r0, r0i), (i0, i0i), (r1, r1i), (i1, i1i) = (
        (spec[32 * i : 32 * i + 32, :128], spec[32 * i : 32 * i + 32, 128:]) for i in range(4)
    )
    first = jnp.concatenate(
        [ar * r0 + br * r1 - (ai * i0i + bi * i1i), ar * r0i + br * r1i + ai * i0 + bi * i1], axis=1
    )
    second = jnp.concatenate(
        [br * r0 + dr * r1 - (bi * i0i + di * i1i), br * r0i + dr * r1i + bi * i0 + di * i1], axis=1
    )
    back = mm3(halves(jnp.concatenate([first, second], axis=0)), ik)
    cs, sn = tw2[0], tw2[1]
    main, rim = [], []
    for c in range(2):
        re = back[32 * c : 32 * c + 32, :256]
        im = back[32 * c : 32 * c + 32, 256:]
        value = jnp.concatenate([re * cs - im * sn, re * sn + im * cs], axis=0)
        main.append(value[:, :128])
        rim.append(value[:, 128:136])
    stack = jnp.concatenate(main + rim + [jnp.zeros((64, 112), F32)], axis=1)
    out = mm3(d2, halves(stack))
    even = lax.broadcasted_iota(jnp.int32, (64, 384), 0) % 2 == 0
    return jnp.concatenate(
        [(out + jnp.where(even, columns[2 * y : 2 * y + 1], columns[2 * y + 1 : 2 * y + 2])).astype(BF) for y in range(4)],
        axis=0,
    )


def regroup(lines):
    a = lax.broadcasted_iota(jnp.int32, (64, 64), 0)
    b = lax.broadcasted_iota(jnp.int32, (64, 64), 1)
    eye = jnp.where(a == b, 1.0, 0.0).astype(BF)
    turned = mm(lines, eye, 0, 0)
    main = jnp.concatenate(
        [
            jnp.concatenate([turned[32 * j : 32 * j + 32] for j in range(4)], axis=1),
            jnp.concatenate([turned[128 + 32 * j : 160 + 32 * j] for j in range(4)], axis=1),
        ],
        axis=0,
    )
    rim = jnp.concatenate(
        [jnp.concatenate([turned[256 + 8 * c + 2 * j : 258 + 8 * c + 2 * j] for j in range(4)], axis=1) for c in range(2)],
        axis=0,
    )
    return jnp.concatenate([main, rim, jnp.zeros((4, 256), F32)], axis=0).astype(BF)


def y_inverse(got, turn, zero, tk):
    lane = lax.broadcasted_iota(jnp.int32, (1, 384), 1)
    odd = (lane % 2).astype(F32)
    acc = [None] * 4
    for e in range(4):
        lines = regroup(got[e])
        part = mm(lines, tk)
        re, im = part[:, :384], part[:, 384:]
        if e == 0:
            own = lines.astype(F32)
            once = zero * (own[:, 1:2] * (1.0 - 2.0 * odd) - own[:, 0:1])
        for d in range(4):
            i = 4 * e + d
            piece = re * turn[0, i : i + 1] - im * turn[1, i : i + 1]
            acc[d] = piece + once if e == 0 else acc[d] + piece
    return jnp.concatenate(acc, axis=0)


def activations(pieces, above, center, below, point, lift18):
    mix = lax.dot_general(point, lift18, (((1,), (0,)), ((), ())), precision=lax.Precision.HIGHEST, preferred_element_type=F32)
    mix_hi, mix_lo = halves(mix)
    mix3 = jnp.concatenate([mix_hi, mix_lo, mix_hi], axis=1)
    a = lax.broadcasted_iota(jnp.int32, (64, 64), 0)
    b = lax.broadcasted_iota(jnp.int32, (64, 64), 1)
    eye = jnp.where(a == b, 1.0, 0.0).astype(BF)
    lines = jnp.concatenate([p.astype(F32)[:, 272:336] for p in pieces] + [jnp.zeros((4, 64), F32)], axis=0)
    turned = mm(eye, lines.astype(BF), 1, 1)
    moved = []
    for s in range(2):
        rows = turned[32 * s : 32 * s + 32]

        def side(k):
            return jnp.concatenate(
                [rows[30:, 2 * k : 2 * k + 2], rows[:, 2 * k + 2 : 2 * k + 4], rows[:2, 2 * k + 4 : 2 * k + 6]], axis=0
            )

        mid = jnp.concatenate([above[s], center[32 * s : 32 * s + 32], below[s]], axis=0)
        full = jnp.concatenate([mid, side(3), jnp.zeros((36, 124), F32), side(0)], axis=1)
        moved.append(jnp.concatenate([full[:, 383:], full[:, :383]], axis=1))
        moved.append(full)
        moved.append(jnp.concatenate([full[:, 1:], full[:, :1]], axis=1))
    blocks = [
        jnp.concatenate([m[r : r + 1] for m in moved] + [jnp.zeros((2, 384), F32)], axis=0) for r in range(36)
    ]
    result = []
    for i in range(34):
        view, view_lo = halves(jnp.concatenate(blocks[i : i + 3], axis=0))
        result.append(jnp.tanh(mm(mix3, jnp.concatenate([view, view, view_lo], axis=0))).astype(BF))
    mix2 = mix3[:, :48]
    return jnp.concatenate(blocks, axis=0), jnp.concatenate(result, axis=0), jnp.concatenate([mix2, mix2], axis=0)


def network(proj, planes, squash, mix4, center, out_cols):
    taps = [None] * 34
    sums = jnp.zeros((56, 128), F32)
    rest = jnp.zeros((56, 64), F32)
    for i in range(-1, 33):
        t_b = squash[(i + 1) * 64 : (i + 2) * 64]
        t = t_b.astype(F32)
        ids = (64, 66) if i < 0 else (65, 67) if i >= 32 else (i, 32 + i)
        g0 = proj[ids[0] : ids[0] + 1]
        g1 = proj[ids[1] : ids[1] + 1]
        grad = out_cols[:, 0:1] * g0 + out_cols[:, 1:2] * g1
        gz, gz_lo = halves(grad * (1.0 - t * t))
        tap = mm(mix4, jnp.concatenate([gz, gz_lo], axis=0), 0, 0)
        tap = tap[:24] + tap[24:]
        for a in range(3):
            k = i + a - 1
            if 0 <= k < 32:
                piece = tap[a * 8 : a * 8 + 8]
                taps[k] = piece if taps[k] is None else taps[k] + piece
        if 0 <= i < 32:
            view, view_lo = halves(planes[(i + 1) * 8 : (i + 4) * 8, :256])
            g_hi, g_lo = halves(jnp.concatenate([g0[:, :256], g1[:, :256]], axis=0))
            g8 = jnp.concatenate([g_hi.astype(F32), g_lo.astype(F32), jnp.zeros((4, 256), F32)], axis=0).astype(BF)
            left = jnp.concatenate([view, view_lo, g8], axis=0)
            sums = sums + mm(left, jnp.concatenate([gz[:, :256], t_b[:, :256]], axis=0), 1, 1)
            rest = rest + mm(left, gz_lo[:, :256], 1, 1)
    tail = sums[48:50, 64:] + sums[50:52, 64:]
    tail = jnp.concatenate([tail, jnp.zeros((6, 64), F32)], axis=0)
    sums = sums[:24, :64] + sums[24:48, :64] + (rest[:24] + rest[24:48])
    row = lax.broadcasted_iota(jnp.int32, (8, 64), 0)
    lane = lax.broadcasted_iota(jnp.int32, (8, 64), 1)
    for s in range(2):
        for v in range(2):
            prod = proj[32 * s : 32 * s + 32, :256] * center[32 * v : 32 * v + 32]
            total = jnp.sum(jnp.sum(prod, axis=0, keepdims=True), axis=1, keepdims=True)
            tail = jnp.where((row == 2) & (lane == 2 * s + v), total, tail)
    packed = jnp.concatenate(
        [
            jnp.concatenate([sums[0:8], sums[8:16]], axis=1),
            jnp.concatenate([sums[16:24], tail], axis=1),
        ],
        axis=0,
    )
    return jnp.concatenate(taps[:32], axis=0), jnp.concatenate([packed] * 16, axis=0)


def call(body, out_shapes, *args):
    single = not isinstance(out_shapes, (tuple, list))

    def kernel(*refs):
        ins = [ref[...] for ref in refs[: len(args)]]
        outs = body(*ins)
        for ref, value in zip(refs[len(args) :], [outs] if single else outs):
            ref[...] = value

    return pl.pallas_call(
        kernel,
        out_shape=out_shapes,
        compiler_params=pltpu.CompilerParams(vmem_limit_bytes=12 * 1024 * 1024),
    )(*args)


def call_picked(body, out_shapes, index, picked, *args):
    def kernel(index_ref, picked_ref, *refs):
        pieces = [picked_ref[index_ref[k]] for k in range(index.shape[0])]
        outs = body(pieces, *[ref[...] for ref in refs[: len(args)]])
        for ref, value in zip(refs[len(args) :], outs):
            ref[...] = value

    vmem = pl.BlockSpec(memory_space=pltpu.VMEM)
    return pl.pallas_call(
        kernel,
        in_specs=[pl.BlockSpec(memory_space=pltpu.SMEM)] + [vmem] * (1 + len(args)),
        out_specs=[vmem] * len(out_shapes),
        out_shape=out_shapes,
        compiler_params=pltpu.CompilerParams(vmem_limit_bytes=12 * 1024 * 1024),
    )(index, picked, *args)


def sds(shape, dtype):
    return jax.ShapeDtypeStruct(shape, dtype)


def exchange(value, axes):
    return lax.all_to_all(value, axes, split_axis=0, concat_axis=0)


def from_row_neighbour(value, step):
    return lax.ppermute(value, IN_W, [(i, (i + step) % WA) for i in range(WA)])


def pack_first(vel, cotangent):
    def kernel(vel_ref, cot_ref, out_ref, rows_ref, cells_ref, sems):
        first = pltpu.make_async_copy(vel_ref, rows_ref, sems.at[0])
        second = pltpu.make_async_copy(cot_ref, cells_ref, sems.at[1])
        first.start()
        second.start()
        first.wait()
        second.wait()
        rows = rows_ref[...]
        edges = jnp.concatenate([rows[:, 0:2], rows[:, 254:256], jnp.zeros((64, 124), F32)], axis=1).T[:8]
        edges = jnp.concatenate([edges, jnp.zeros((8, 192), F32)], axis=1)
        cells = cells_ref[...]
        for d in range(4):
            out_ref[d, :64] = cells
            out_ref[d, 64:] = edges

    anywhere = pl.BlockSpec(memory_space=pl.ANY)
    return pl.pallas_call(
        kernel,
        in_specs=[anywhere, anywhere],
        out_specs=pl.BlockSpec(memory_space=pltpu.VMEM),
        out_shape=sds((4, 72, 256), F32),
        scratch_shapes=[pltpu.VMEM((64, 256), F32), pltpu.VMEM((64, 256), F32), pltpu.SemaphoreType.DMA((2,))],
    )(vel, cotangent)


def sum_and_spread(got):
    total = got[0]
    for i in range(1, 16):
        total = total + got[i]
    return jnp.concatenate([total] * 32, axis=0)


def turns(own, cols):
    ang = TWO_PI / NY * (own * cols % NY).astype(F32)
    return jnp.stack([jnp.cos(ang), jnp.sin(ang)])


def columns_to_send(got, x, yl):
    def edges(src, first):
        rows = lax.dynamic_index_in_dim(got, src, 0, False)
        return rows[64 + first : 66 + first, :64]

    up = edges(jnp.where(yl == 3, (x + 3) % 4, x), 2)
    down = edges(jnp.where(yl == 0, (x + 1) % 4, x), 0)
    to_y = jnp.arange(4)[:, None, None]
    cols = jnp.where(to_y == (yl + 1) % 4, up, down)
    return jnp.pad(cols.reshape(8, 64), ((0, 0), (272, 48)))


def lift_matrix(lift, kernels):
    parts = []
    for a in range(3):
        for s in range(2):
            for b in range(3):
                parts.append(kernels[:, 3 * a + b] * lift[:, s])
        parts += [jnp.zeros_like(parts[0])] * 2
    return jnp.stack(parts, axis=1)


def finish_velocity(proj, taps, lift, out_w):
    hi = lax.Precision.HIGHEST
    main = proj[:64, :256].reshape(2, 32, 256)
    m2 = jnp.dot(lift.T, out_w.astype(F32).T, precision=hi)
    taps = taps.reshape(32, 8, 384)
    out = []
    for s in range(2):
        left, mid, right = taps[:, 3 * s], taps[:, 3 * s + 1], taps[:, 3 * s + 2]
        value = main[s] + m2[s, 0] * main[0] + m2[s, 1] * main[1] + mid[:, :256]
        value = value + jnp.concatenate([right[:, 383:], right[:, :255]], axis=1)
        value = value + left[:, 1:257]
        out.append(value)
    return jnp.stack(out)


def finish_weights(got, lift_rows, kernel_rows, point, out_rows, lift18_rows):
    hi = lax.Precision.HIGHEST
    total = got[0]
    for i in range(1, 32):
        total = total + got[i]
    total = total * (1.0 / math.sqrt(NX * NY))
    q = jnp.concatenate([total[:8, :64], total[:8, 64:], total[8:, :64]], axis=0)

    def pair_sum(s, v):
        return total[10:11, 64 + 2 * s + v : 65 + 2 * s + v]

    grad_out = [
        total[8 + s : 9 + s, 64:] + pair_sum(s, 0) * lift_rows[0:1] + pair_sum(s, 1) * lift_rows[1:2] for s in range(2)
    ]
    grad_point = lax.dot_general(q, lift18_rows, (((0,), (0,)), ((), ())), precision=hi, preferred_element_type=F32)
    gv = lax.dot_general(q, point, (((1,), (0,)), ((), ())), precision=hi, preferred_element_type=F32)
    grad_kernels = [
        lift_rows[0:1] * gv[8 * a : 8 * a + 3] + lift_rows[1:2] * gv[8 * a + 3 : 8 * a + 6] for a in range(3)
    ]
    grad_lift = []
    for s in range(2):
        value = out_rows[0:1] * pair_sum(0, s) + out_rows[1:2] * pair_sum(1, s)
        for a in range(3):
            first = 8 * a + 3 * s
            value = value + jnp.sum(kernel_rows[3 * a : 3 * a + 3] * gv[first : first + 3], axis=0, keepdims=True)
        grad_lift.append(value)
    return (
        jnp.concatenate(grad_lift, axis=0),
        jnp.concatenate(grad_kernels, axis=0).reshape(9, 1, 64),
        grad_point,
        jnp.concatenate(grad_out, axis=0),
    )


def local(velocity, cotangent, lift_weight, depth_kernels, point_weights, out_weight):
    tab = make_tables()
    x, yl, yh, z, core = (lax.axis_index(a) for a in AXES)
    w = 16 * yh + 2 * z + core
    kernels = depth_kernels[0]
    point = point_weights[0]
    col = jnp.arange(256)[None, :]
    step = jnp.arange(16)[:, None]
    klass = x + 4 * (step // 4)
    turn1 = turns(klass, col + 1024 * (step % 4) + 256 * yl)
    sign = jnp.where(x == 0, (1 - 2 * (col % 2)).astype(F32), 0.0)
    zero = jnp.where(x == 0, jnp.ones((1, 384), F32), 0.0)
    ky_lane = (x + 4 * yl + 16 * (4 * w + jnp.arange(128) // 32)).astype(F32)[None, :]
    cols4 = jnp.asarray(COL_ID.astype(np.int32))[None, :]
    turn4 = turns(klass, cols4 + 1024 * (step % 4) + 256 * yl + NY)
    lift18 = lift_matrix(lift_weight, kernels)

    got1 = exchange(pack_first(velocity.reshape(64, 256), cotangent.reshape(64, 256)), ("x",))
    spec = call(y_forward, sds((128, 2, 256), F32), got1, turn1, sign, tab["t1"])
    spec, bottom = lax.optimization_barrier((spec, velocity[:, 30:]))
    got2 = exchange(spec, ("yl",) + IN_W)
    above = from_row_neighbour(bottom, 1)
    columns = columns_to_send(got1, x, yl)
    sent3 = call(
        x_project, sds((256, 384), BF), got2.reshape(4, 64, 256), ky_lane, columns, tab["d1"], tab["tw1"], tab["kr"], tab["ik"], tab["tw2"], tab["d2"]
    )
    sent3, above, top = lax.optimization_barrier((sent3, above, velocity[:, :2]))
    below = from_row_neighbour(top, -1)
    got3 = exchange(sent3.reshape(128, 2, 384), ("yl",) + IN_W)
    sent4 = call(y_inverse, sds((288, 384), F32), got3.reshape(4, 64, 384), turn4, zero, tab["tk"])
    sent4, below = lax.optimization_barrier((sent4, below))
    got4 = exchange(sent4.reshape(4, 72, 384), ("x",))
    point_f = point.astype(F32)
    out_cols = out_weight.astype(F32).T
    center = velocity.reshape(64, 256)
    near = [((yl + dy) % 4) * WA + (w + dw) % WA for dy in (3, 1) for dw in (31, 0, 1)]
    planes, squash, mix4 = call_picked(
        activations,
        (sds((288, 384), F32), sds((34 * 64, 384), BF), sds((128, 48), BF)),
        jnp.stack(near).astype(jnp.int32), got3, above, center, below, point_f, lift18,
    )

    def last(got, *rest):
        proj = (got[0] + got[1]) + (got[2] + got[3])
        return (proj,) + network(proj, *rest)

    proj, taps, packed = call(
        last,
        (sds((72, 384), F32), sds((256, 384), F32), sds((256, 128), F32)),
        got4, planes, squash, mix4, center, out_cols,
    )
    part = exchange(packed.reshape(16, 16, 128), ("yl", "yh", "c"))
    part = call(sum_and_spread, sds((512, 128), F32), part)
    total = exchange(part.reshape(32, 16, 128), ("x", "z"))
    grad_velocity = finish_velocity(proj, taps, lift_weight, out_weight)
    grad_lift, grad_kernels, grad_point, grad_out = call(
        finish_weights,
        (sds((2, 64), F32), sds((9, 1, 64), F32), sds((64, 64), F32), sds((2, 64), F32)),
        total, lift_weight.T, kernels.T, point_f, out_weight.astype(F32), lift18.T,
    )
    return grad_velocity, grad_lift.T, grad_kernels.transpose(1, 2, 0), grad_point[None], grad_out


def solution(mesh):
    split = jax.sharding.Mesh(mesh.devices.reshape(SIZES), AXES)
    field = P(None, IN_W, IN_H)
    return jax.shard_map(
        local,
        mesh=split,
        in_specs=(field, field, P(), P(), P(), P()),
        out_specs=(field, P(), P(), P(), P()),
        check_vma=False,
    )
```
